32 devices in a mesh: groups: 2 (over x), seq: 8 (over z, y), chan: 2 (over core).
Axes of the slice: x: 2, y: 2, z: 4, core: 2. Of those that a mesh axis runs over, the one named last changes fastest.
Arguments:
- inputs: bfloat16 [8192, 768], P(('groups', 'seq')), parts along dimension 0, may hold values from -6 to 6
- enc_weight: bfloat16 [768, 5, 1536], P('seq', None, 'chan'), may hold values from -0.09375 to 0.09375
- dec_weight: bfloat16 [768, 5, 1536], P('seq', None, 'chan'), may hold values from -0.0625 to 0.0625
- cotangent: bfloat16 [8192, 768], P(('groups', 'seq'), 'chan'), parts along dimension 0, may hold values from -6 to 6
Outputs:
- mixed_out: bfloat16 [8192, 768], P(('groups', 'seq'), 'chan'), parts along dimension 0
- input_grad: bfloat16 [8192, 768], P(('groups', 'seq'), 'chan'), parts along dimension 0
- enc_grad: bfloat16 [1536, 5, 1536], P(('groups', 'seq'), None, 'chan'), parts along dimension 0
- dec_grad: bfloat16 [1536, 5, 1536], P(('groups', 'seq'), None, 'chan'), parts along dimension 0
The draws below stay inside these ranges and needn't reach their ends.
There are 2 independent parts, one for each index of `groups`. The reference program is written for one: setup_inputs(seed, part) draws one part's arguments, and reference() takes and returns one part's arrays. A program takes and returns all parts, laid end to end along the dimension named above; an argument that names none is the same for every part. Nothing has to cross between parts.
All inputs are finite; a program needn't handle non-finite values.
Results may differ from the reference program's by a relative error of at most 0.012.
Values may be sent and summed in bfloat16 or wider, within the bound.
A program may use at most 128 MiB of HBM per device.

```python
import jax
import jax.numpy as jnp
from jax import lax

C1 = 768
C2 = 1536
K = 5
R1 = 256
R0 = 512
L1 = 2048
L0 = 4096
N_SEQ = 8


def spiked(array, key, source, target, shards_of, factor):
    owner, partner = [(jnp.arange(array.shape[dim]) // (array.shape[dim] // shards_of)).reshape([-1 if axis == dim else 1 for axis in range(array.ndim)]) for dim in (source, target)]
    chosen = jax.random.permutation(key, shards_of)[partner]
    strong = (owner == chosen) | (owner == (partner + shards_of // 2) % shards_of)
    return jnp.where(strong, factor * array, array)


def block_levels(stream_key, shape, shards, smallest, top_value):
    level = 1.0
    for position, parts in shards:
        steps = jax.random.uniform(jax.random.fold_in(jax.random.fold_in(stream_key, 6), position), (parts,), jnp.float32, smallest / len(shards), top_value / len(shards))
        level = level * jnp.repeat(jnp.exp(steps), shape[position] // parts).reshape((-1,) + (1,) * (len(shape) - 1 - position))
    return level


def noise(stream_key, extent, deviation, bound, cuts=(), held_as=jnp.bfloat16):
    entries = deviation * jax.random.normal(stream_key, extent, jnp.float32)
    if cuts:
        entries = entries * block_levels(stream_key, extent, cuts, -0.22, 0.18)
    return jnp.clip(entries, -bound, bound).astype(held_as)


def bell_draw_with(key, extent, scale, bound, split, heavy, kind=jnp.bfloat16):
    drawn = scale * jax.random.normal(key, extent, jnp.float32)
    if split:
        drawn = drawn * block_levels(key, extent, split, -0.22, 0.18)
    return jnp.clip(spiked(drawn, jax.random.fold_in(key, 3), *heavy), -bound, bound).astype(kind)


def setup_inputs(seed: int = 0, part: int = 0) -> dict:
    key_of = jax.random.split(jax.random.key(seed), 5)
    part_splits = jax.random.split(jax.random.fold_in(key_of[4], part), 5)
    return {
        "inputs": bell_draw_with(part_splits[0], (L0, C1), 1.0, 6.0, ((0, 8),), (0, 1, 8, 2.0)),
        "enc_weight": noise(key_of[1], (C1, K, C2), (K * C1) ** -0.5, 0.09375, ((0, 8), (2, 2))),
        "dec_weight": noise(key_of[2], (C1, K, C2), (K * C2) ** -0.5, 0.0625, ((0, 8), (2, 2))),
        "cotangent": bell_draw_with(part_splits[3], (L0, C1), 1.0, 6.0, ((0, 8), (1, 2)), (0, 1, 8, 2.0)),
    }


def gelu_fn(values):
    return jax.nn.gelu(values, approximate=True)

def reference(inputs, enc_weight, dec_weight, cotangent):
    pooled = (inputs.astype(jnp.float32).reshape(L1, 2, C1).sum(axis=1) * 0.5).astype(jnp.bfloat16)
    pad_pool = jnp.pad(pooled, ((2, 2), (0, 0)))
    pre_act = jnp.zeros((L1, C2), jnp.float32)
    for tap_index in range(K):
        pre_act = pre_act + jnp.dot(pad_pool[tap_index:tap_index + L1], enc_weight[:, tap_index, :], preferred_element_type=jnp.float32)
    hidden = gelu_fn(pre_act).astype(jnp.bfloat16)
    upsampled = jnp.repeat(hidden, 2, axis=0)
    pad_up = jnp.pad(upsampled, ((2, 2), (0, 0)))
    decoded = jnp.zeros((L0, C1), jnp.float32)
    for tap_index in range(K):
        decoded = decoded + lax.dot_general(pad_up[tap_index:tap_index + L0], dec_weight[:, tap_index, :], (((1,), (1,)), ((), ())), preferred_element_type=jnp.float32)
    mixed_out = (inputs.astype(jnp.float32) + decoded).astype(jnp.bfloat16)
    pad_cot = jnp.pad(cotangent, ((2, 2), (0, 0)))
    up_grad = jnp.zeros((L0, C2), jnp.float32)
    for tap_index in range(K):
        up_grad = up_grad + jnp.dot(pad_cot[4 - tap_index:4 - tap_index + L0], dec_weight[:, tap_index, :], preferred_element_type=jnp.float32)
    hid_grad = up_grad.reshape(L1, 2, C2).sum(axis=1)
    _, pullback = jax.vjp(gelu_fn, pre_act)
    pre_grad = pullback(hid_grad)[0].astype(jnp.bfloat16)
    pad_grad = jnp.pad(pre_grad, ((2, 2), (0, 0)))
    pool_grad = jnp.zeros((L1, C1), jnp.float32)
    for tap_index in range(K):
        pool_grad = pool_grad + lax.dot_general(pad_grad[4 - tap_index:4 - tap_index + L1], enc_weight[:, tap_index, :], (((1,), (1,)), ((), ())), preferred_element_type=jnp.float32)
    input_grad = (cotangent.astype(jnp.float32) + 0.5 * jnp.repeat(pool_grad, 2, axis=0)).astype(jnp.bfloat16)

    def add_block(carry, block_index):
        enc_total, dec_total = carry
        coarse_start = (block_index * R1).astype(jnp.int32)
        fine_start = (block_index * R0).astype(jnp.int32)
        block_pool = lax.dynamic_slice_in_dim(pad_pool, coarse_start, R1 + 4, 0)
        block_grad = lax.dynamic_slice_in_dim(pre_grad, coarse_start, R1, 0)
        block_up = lax.dynamic_slice_in_dim(pad_up, fine_start, R0 + 4, 0)
        block_cot = lax.dynamic_slice_in_dim(cotangent, fine_start, R0, 0)
        enc_terms = jnp.stack([jnp.dot(block_pool[tap_index:tap_index + R1].T, block_grad, preferred_element_type=jnp.float32) for tap_index in range(K)], axis=1)
        dec_terms = jnp.stack([jnp.dot(block_cot.T, block_up[tap_index:tap_index + R0], preferred_element_type=jnp.float32) for tap_index in range(K)], axis=1)
        enc_total = enc_total + enc_terms.astype(jnp.bfloat16).astype(jnp.float32)
        dec_total = dec_total + dec_terms.astype(jnp.bfloat16).astype(jnp.float32)
        return ((enc_total, dec_total), None)
    zeros_init = (jnp.zeros((C1, K, C2), jnp.float32), jnp.zeros((C1, K, C2), jnp.float32))
    (enc_total, dec_total), _ = lax.scan(add_block, zeros_init, jnp.arange(N_SEQ, dtype=jnp.int32))
    return (mixed_out, input_grad, enc_total.astype(jnp.bfloat16), dec_total.astype(jnp.bfloat16))
```

```python
import jax
import jax.numpy as jnp
from jax import lax
from jax.sharding import PartitionSpec as P

BF16 = jnp.bfloat16
F32 = jnp.float32


def shift(array, by):
    length = array.shape[0]
    if by == 0:
        return array
    pad = jnp.zeros((abs(by),) + array.shape[1:], array.dtype)
    if by > 0:
        return jnp.concatenate([array[by:], pad], axis=0)
    return jnp.concatenate([pad, array[: length + by]], axis=0)


def to_columns(array, parts):
    rows, cols = array.shape
    blocks = array.reshape(rows, parts, cols // parts).transpose(1, 0, 2)
    return lax.all_to_all(blocks, "seq", 0, 0, tiled=True)


def to_rows(blocks):
    parts, rows, cols = blocks.shape
    got = lax.all_to_all(blocks, "seq", 0, 0, tiled=True)
    return got.transpose(1, 0, 2).reshape(rows, parts * cols)


def gelu_fn(values):
    return jax.nn.gelu(values, approximate=True)


def shards(inputs, enc_weight, dec_weight, cotangent):
    parts = lax.axis_size("seq")
    rows, width = inputs.shape
    half = rows // 2
    total = half * parts
    block, taps, share = enc_weight.shape
    half_width = cotangent.shape[1]

    pooled = (inputs.astype(F32).reshape(half, 2, width).sum(axis=1) * 0.5).astype(BF16)
    cot_full = lax.all_gather(cotangent, "chan", axis=1, tiled=True)
    columns = to_columns(jnp.concatenate([pooled, cot_full], axis=0), parts)
    pool_col = columns[:, :half].reshape(total, block)
    cot_col = columns[:, half:].reshape(total, 2, block).astype(F32)
    even = cot_col[:, 0]
    odd = cot_col[:, 1]
    pair = (even + odd).astype(BF16)
    cross = (odd + shift(even, 1)).astype(BF16)
    before = jnp.concatenate([even[:1].astype(BF16), cross[:-1]], axis=0)
    pool_taps = jnp.concatenate([shift(pool_col, t - 2) for t in range(taps)], axis=1)
    cot_taps = jnp.concatenate([shift(pair, 1), cross, pair, before, shift(pair, -1)], axis=1)
    enc_mat = enc_weight.transpose(1, 0, 2).reshape(taps * block, share)
    dec_mat = dec_weight.transpose(1, 0, 2).reshape(taps * block, share)

    partial = jnp.concatenate(
        [
            jnp.dot(pool_taps, enc_mat, preferred_element_type=F32).astype(BF16),
            jnp.dot(cot_taps, dec_mat, preferred_element_type=F32).astype(BF16),
        ],
        axis=1,
    )
    summed = lax.psum_scatter(partial, "seq", scatter_dimension=0, tiled=True).astype(F32)
    pre_act = summed[:, :share]
    hid_grad = summed[:, share:]
    hidden, pullback = jax.vjp(gelu_fn, pre_act)
    pre_grad = pullback(hid_grad)[0].astype(BF16)
    joint = jnp.concatenate([hidden.astype(BF16), pre_grad], axis=1)
    joint = lax.all_gather(joint, "seq", axis=0, tiled=True)
    hidden_all = joint[:, :share]
    grad_all = joint[:, share:]

    contract_rows = (((0,), (0,)), ((), ()))
    contract_last = (((1,), (1,)), ((), ()))
    dec_grad = lax.dot_general(cot_taps, hidden_all, contract_rows, preferred_element_type=F32)
    enc_grad = lax.dot_general(pool_taps, grad_all, contract_rows, preferred_element_type=F32)
    dec_grad = dec_grad.astype(BF16).reshape(taps, block, share).transpose(1, 0, 2)
    enc_grad = enc_grad.astype(BF16).reshape(taps, block, share).transpose(1, 0, 2)

    dec_out = lax.dot_general(hidden_all, dec_mat, contract_last, preferred_element_type=F32)
    p0, p1, p2, p3, p4 = [dec_out[:, t * block : (t + 1) * block] for t in range(taps)]
    after4 = shift(p4, 1)
    before0 = shift(p0, -1)
    dec_even = before0 + shift(p1, -1) + p2 + p3 + after4
    dec_odd = before0 + p1 + p2 + shift(p3, 1) + after4
    decoded = jnp.stack([dec_even, dec_odd], axis=1).astype(BF16).reshape(parts, rows, block)
    enc_out = lax.dot_general(grad_all, enc_mat, contract_last, preferred_element_type=F32)
    pool_grad = sum(shift(enc_out[:, t * block : (t + 1) * block], 2 - t) for t in range(taps))
    pool_grad = pool_grad.astype(BF16).reshape(parts, half, block)
    mine = to_rows(jnp.concatenate([decoded, pool_grad], axis=1))
    mine = lax.psum_scatter(mine, "chan", scatter_dimension=1, tiled=True).astype(F32)

    col_start = lax.axis_index("chan") * half_width
    skip = lax.dynamic_slice_in_dim(inputs, col_start, half_width, 1)
    mixed_out = (skip.astype(F32) + mine[:rows]).astype(BF16)
    input_grad = (cotangent.astype(F32) + 0.5 * jnp.repeat(mine[rows:], 2, axis=0)).astype(BF16)
    return mixed_out, input_grad, enc_grad, dec_grad


def solution(mesh):
    return jax.shard_map(
        shards,
        mesh=mesh,
        in_specs=(
            P(("groups", "seq"), None),
            P("seq", None, "chan"),
            P("seq", None, "chan"),
            P(("groups", "seq"), "chan"),
        ),
        out_specs=(
            P(("groups", "seq"), "chan"),
            P(("groups", "seq"), "chan"),
            P(("groups", "seq"), None, "chan"),
            P(("groups", "seq"), None, "chan"),
        ),
        check_vma=False,
    )
```

```python
import functools
import math

import jax
import jax.numpy as jnp
from jax import lax
from jax.experimental import pallas as pl
from jax.experimental.pallas import tpu as pltpu
from jax.sharding import PartitionSpec as P

BF16 = jnp.bfloat16
F32 = jnp.float32


def shift(array, by):
    length = array.shape[0]
    if by == 0:
        return array
    pad = jnp.zeros((abs(by),) + array.shape[1:], array.dtype)
    if by > 0:
        return jnp.concatenate([array[by:], pad], axis=0)
    return jnp.concatenate([pad, array[: length + by]], axis=0)


def to_columns(array, parts):
    rows, cols = array.shape
    blocks = array.reshape(rows, parts, cols // parts).transpose(1, 0, 2)
    return lax.all_to_all(blocks, "seq", 0, 0, tiled=True)


def to_rows(blocks):
    parts, rows, cols = blocks.shape
    got = lax.all_to_all(blocks, "seq", 0, 0, tiled=True)
    return got.transpose(1, 0, 2).reshape(rows, parts * cols)


PIECES = 2


def ring_place(index, n):
    if n != 8:
        return index
    y = lax.rem(index, 2)
    z = index // 2
    return z + y * (n - 1 - 2 * z)


def ring_index(place, n):
    place = lax.rem(place + 2 * n, n)
    if n != 8:
        return place
    back = place // (n // 2)
    return 2 * place + back * (2 * n - 1 - 4 * place)


def gelu_and_slope(v):
    scale = math.sqrt(2.0 / math.pi)
    square = v * v
    th = jnp.tanh(scale * (v + 0.044715 * square * v))
    up = 0.5 * (1.0 + th)
    slope = up + 0.5 * v * (1.0 - th * th) * (scale * (1.0 + 3.0 * 0.044715 * square))
    return v * up, slope


def ring_kernel(
    n, x_ref, y_ref, enc_ref, dec_ref, out_ref, slots, term, mine,
    rs_send, rs_recv, ag_send, ag_recv, local_sem,
):
    me = lax.axis_index("seq")
    place = ring_place(me, n)
    nexts = (ring_index(place + 1, n), ring_index(place - 1, n))
    half = x_ref.shape[1]
    share = enc_ref.shape[1]
    side = half // 2
    piece = side // PIECES

    barrier = pltpu.get_barrier_semaphore()
    for other in nexts:
        pl.semaphore_signal(
            barrier, inc=1, device_id={"seq": other}, device_id_type=pl.DeviceIdType.MESH
        )
    pl.semaphore_wait(barrier, 2)

    def signed(d, steps):
        return place - steps if d == 0 else place + steps

    def own_term(d, steps):
        chunk = ring_index(signed(d, steps), n)
        at = pl.ds(d * side, side)
        a = jnp.dot(x_ref[chunk, at, :], enc_ref[...], preferred_element_type=jnp.float32)
        b = jnp.dot(y_ref[chunk, at, :], dec_ref[...], preferred_element_type=jnp.float32)
        return a, b

    def rs_copy(d, s, q):
        at = pl.ds(q * piece, piece)
        return pltpu.make_async_remote_copy(
            src_ref=slots.at[d, s, at],
            dst_ref=slots.at[d, s + 1, at],
            send_sem=rs_send.at[d, s, q],
            recv_sem=rs_recv.at[d, s, q],
            device_id={"seq": nexts[d]},
            device_id_type=pl.DeviceIdType.MESH,
        )

    def ag_copy(d, s, q, first):
        at = pl.ds(d * side + q * piece, piece)
        owner = ring_index(signed(d, s), n)
        return pltpu.make_async_remote_copy(
            src_ref=mine.at[at] if first else out_ref.at[owner, at],
            dst_ref=out_ref.at[owner, at],
            send_sem=ag_send.at[d, s, q],
            recv_sem=ag_recv.at[d, s, q],
            device_id={"seq": nexts[d]},
            device_id_type=pl.DeviceIdType.MESH,
        )

    for d in range(2):
        a, b = own_term(d, 1)
        slots[d, 0, :, :share] = a.astype(BF16)
        slots[d, 0, :, share:] = b.astype(BF16)
        for q in range(PIECES):
            rs_copy(d, 0, q).start()

    def fill(s):
        for d in range(2):
            a, b = own_term(d, s + 2)
            term[d, :, :share] = a
            term[d, :, share:] = b

    def rs_step(s, carry):
        fill(s)
        for q in range(PIECES):
            at = pl.ds(q * piece, piece)
            for d in range(2):
                rs_copy(d, s, q).wait_recv()
                total = slots[d, s + 1, at, :].astype(F32) + term[d, at, :]
                slots[d, s + 1, at, :] = total.astype(BF16)
                rs_copy(d, s + 1, q).start()
        return carry

    lax.fori_loop(0, n - 2, rs_step, 0)
    fill(n - 2)
    for q in range(PIECES):
        at = pl.ds(q * piece, piece)
        for d in range(2):
            rs_copy(d, n - 2, q).wait_recv()
            rows = pl.ds(d * side + q * piece, piece)
            pre = slots[d, n - 1, at, :share].astype(F32) + term[d, at, :share]
            grad = slots[d, n - 1, at, share:].astype(F32) + term[d, at, share:]
            value, slope = gelu_and_slope(pre)
            mine[rows, :share] = value.astype(BF16)
            mine[rows, share:] = (grad * slope).astype(BF16)
            ag_copy(d, 0, q, True).start()
    local = pltpu.make_async_copy(mine, out_ref.at[me], local_sem)
    local.start()

    def ag_step(s, carry):
        for q in range(PIECES):
            for d in range(2):
                incoming(d, s, q).wait_recv()
                ag_copy(d, s + 1, q, False).start()
        return carry

    def incoming(d, s, q):
        at = pl.ds(d * side + q * piece, piece)
        owner = ring_index(signed(d, s + 1), n)
        return pltpu.make_async_remote_copy(
            src_ref=mine.at[at],
            dst_ref=out_ref.at[owner, at],
            send_sem=ag_send.at[d, s, q],
            recv_sem=ag_recv.at[d, s, q],
            device_id={"seq": nexts[d]},
            device_id_type=pl.DeviceIdType.MESH,
        )

    lax.fori_loop(0, n - 2, ag_step, 0)
    for q in range(PIECES):
        for d in range(2):
            incoming(d, n - 2, q).wait_recv()

    def drain(s, carry):
        for q in range(PIECES):
            for d in range(2):
                rs_copy(d, s, q).wait_send()
                ag_copy(d, s, q, True).wait_send()
        return carry

    lax.fori_loop(0, n - 1, drain, 0)
    local.wait()


def ring(pool_taps, cot_taps, enc_mat, dec_mat, n):
    half = pool_taps.shape[1]
    share = enc_mat.shape[1]
    depth = enc_mat.shape[0]
    vmem = pl.BlockSpec(memory_space=pltpu.VMEM)
    steps = (2, n - 1, PIECES)
    return pl.pallas_call(
        functools.partial(ring_kernel, n),
        out_shape=jax.ShapeDtypeStruct((n, half, 2 * share), BF16),
        in_specs=[vmem] * 4,
        out_specs=pl.BlockSpec(memory_space=pl.ANY),
        scratch_shapes=[
            pltpu.VMEM((2, n, half // 2, 2 * share), BF16),
            pltpu.VMEM((2, half // 2, 2 * share), F32),
            pltpu.VMEM((half, 2 * share), BF16),
            pltpu.SemaphoreType.DMA(steps),
            pltpu.SemaphoreType.DMA(steps),
            pltpu.SemaphoreType.DMA(steps),
            pltpu.SemaphoreType.DMA(steps),
            pltpu.SemaphoreType.DMA,
        ],
        compiler_params=pltpu.CompilerParams(
            collective_id=0, has_side_effects=True, vmem_limit_bytes=48 * 2**20
        ),
        cost_estimate=pl.CostEstimate(
            flops=4 * n * half * depth * share,
            bytes_accessed=4 * n * half * share * 2,
            transcendentals=half * share,
        ),
    )(pool_taps, cot_taps, enc_mat, dec_mat)


def shards(inputs, enc_weight, dec_weight, cotangent):
    parts = lax.axis_size("seq")
    rows, width = inputs.shape
    half = rows // 2
    total = half * parts
    block, taps, share = enc_weight.shape
    half_width = cotangent.shape[1]

    pooled = (inputs.astype(F32).reshape(half, 2, width).sum(axis=1) * 0.5).astype(BF16)
    cot_full = lax.all_gather(cotangent, "chan", axis=1, tiled=True)
    core = lax.axis_index("chan")
    cores = lax.axis_size("chan")
    few = half // cores
    leaving = jnp.concatenate(
        [
            lax.dynamic_slice_in_dim(pooled, core * few, few, 0),
            lax.dynamic_slice_in_dim(cot_full, core * 2 * few, 2 * few, 0),
        ],
        axis=0,
    )
    columns = to_columns(leaving, parts).reshape(parts, 1, 3 * few, block)
    columns = lax.all_gather(columns, "chan", axis=1, tiled=True)
    pool_col = columns[:, :, :few].reshape(total, block)
    cot_col = columns[:, :, few:].reshape(total, 2, block).astype(F32)
    even = cot_col[:, 0]
    odd = cot_col[:, 1]
    pair = (even + odd).astype(BF16)
    cross = (odd + shift(even, 1)).astype(BF16)
    before = jnp.concatenate([even[:1].astype(BF16), cross[:-1]], axis=0)
    pool_taps = jnp.concatenate([shift(pool_col, t - 2) for t in range(taps)], axis=1)
    cot_taps = jnp.concatenate([shift(pair, 1), cross, pair, before, shift(pair, -1)], axis=1)
    enc_mat = enc_weight.transpose(1, 0, 2).reshape(taps * block, share)
    dec_mat = dec_weight.transpose(1, 0, 2).reshape(taps * block, share)

    joint = ring(
        pool_taps.reshape(parts, half, taps * block),
        cot_taps.reshape(parts, half, taps * block),
        enc_mat,
        dec_mat,
        parts,
    ).reshape(total, 2 * share)
    hidden_all = joint[:, :share]
    grad_all = joint[:, share:]

    contract_rows = (((0,), (0,)), ((), ()))
    contract_last = (((1,), (1,)), ((), ()))
    dec_grad = lax.dot_general(cot_taps, hidden_all, contract_rows, preferred_element_type=F32)
    enc_grad = lax.dot_general(pool_taps, grad_all, contract_rows, preferred_element_type=F32)
    dec_grad = dec_grad.astype(BF16).reshape(taps, block, share).transpose(1, 0, 2)
    enc_grad = enc_grad.astype(BF16).reshape(taps, block, share).transpose(1, 0, 2)

    dec_out = lax.dot_general(hidden_all, dec_mat, contract_last, preferred_element_type=F32)
    p0, p1, p2, p3, p4 = [dec_out[:, t * block : (t + 1) * block] for t in range(taps)]
    after4 = shift(p4, 1)
    before0 = shift(p0, -1)
    dec_even = before0 + shift(p1, -1) + p2 + p3 + after4
    dec_odd = before0 + p1 + p2 + shift(p3, 1) + after4
    decoded = jnp.stack([dec_even, dec_odd], axis=1).astype(BF16).reshape(parts, rows, block)
    enc_out = lax.dot_general(grad_all, enc_mat, contract_last, preferred_element_type=F32)
    pool_grad = sum(shift(enc_out[:, t * block : (t + 1) * block], 2 - t) for t in range(taps))
    pool_grad = pool_grad.astype(BF16).reshape(parts, half, block)
    mine = jnp.concatenate([decoded, pool_grad], axis=1)
    mine = lax.psum_scatter(mine, "chan", scatter_dimension=1, tiled=True)
    mine = lax.all_gather(to_rows(mine), "chan", axis=0, tiled=True)
    col_start = core * half_width
    mine = lax.dynamic_slice_in_dim(mine, col_start, half_width, 1).astype(F32)

    skip = lax.dynamic_slice_in_dim(inputs, col_start, half_width, 1)
    mixed_out = (skip.astype(F32) + mine[:rows]).astype(BF16)
    input_grad = (cotangent.astype(F32) + 0.5 * jnp.repeat(mine[rows:], 2, axis=0)).astype(BF16)
    return mixed_out, input_grad, enc_grad, dec_grad


def solution(mesh):
    return jax.shard_map(
        shards,
        mesh=mesh,
        in_specs=(
            P(("groups", "seq"), None),
            P("seq", None, "chan"),
            P("seq", None, "chan"),
            P(("groups", "seq"), "chan"),
        ),
        out_specs=(
            P(("groups", "seq"), "chan"),
            P(("groups", "seq"), "chan"),
            P(("groups", "seq"), None, "chan"),
            P(("groups", "seq"), None, "chan"),
        ),
        check_vma=False,
    )
```

```python
import functools
import math

import jax
import jax.numpy as jnp
from jax import lax
from jax.experimental import pallas as pl
from jax.experimental.pallas import tpu as pltpu
from jax.sharding import PartitionSpec as P

BF16 = jnp.bfloat16
F32 = jnp.float32


def shift(array, by):
    length = array.shape[0]
    if by == 0:
        return array
    pad = jnp.zeros((abs(by),) + array.shape[1:], array.dtype)
    if by > 0:
        return jnp.concatenate([array[by:], pad], axis=0)
    return jnp.concatenate([pad, array[: length + by]], axis=0)


def to_columns(array, parts):
    rows, cols = array.shape
    blocks = array.reshape(rows, parts, cols // parts).transpose(1, 0, 2)
    return lax.all_to_all(blocks, "seq", 0, 0, tiled=True)


def to_rows(blocks):
    parts, rows, cols = blocks.shape
    got = lax.all_to_all(blocks, "seq", 0, 0, tiled=True)
    return got.transpose(1, 0, 2).reshape(rows, parts * cols)


PIECES = 2


def ring_place(index, n):
    if n != 8:
        return index
    y = lax.rem(index, 2)
    z = index // 2
    return z + y * (n - 1 - 2 * z)


def ring_index(place, n):
    place = lax.rem(place + 2 * n, n)
    if n != 8:
        return place
    back = place // (n // 2)
    return 2 * place + back * (2 * n - 1 - 4 * place)


def gelu_and_slope(v):
    scale = math.sqrt(2.0 / math.pi)
    square = v * v
    th = jnp.tanh(scale * (v + 0.044715 * square * v))
    up = 0.5 * (1.0 + th)
    slope = up + 0.5 * v * (1.0 - th * th) * (scale * (1.0 + 3.0 * 0.044715 * square))
    return v * up, slope


def ring_kernel(
    n, x_ref, y_ref, enc_ref, dec_ref, out_ref, slots, term, mine,
    rs_send, rs_recv, ag_send, ag_recv, local_sem,
):
    me = lax.axis_index("seq")
    place = ring_place(me, n)
    nexts = (ring_index(place + 1, n), ring_index(place - 1, n))
    half = x_ref.shape[1]
    share = enc_ref.shape[1]
    side = half // 2
    piece = side // PIECES

    barrier = pltpu.get_barrier_semaphore()
    for other in nexts:
        pl.semaphore_signal(
            barrier, inc=1, device_id={"seq": other}, device_id_type=pl.DeviceIdType.MESH
        )
    pl.semaphore_wait(barrier, 2)

    def signed(d, steps):
        return place - steps if d == 0 else place + steps

    def own_term(d, steps):
        chunk = ring_index(signed(d, steps), n)
        at = pl.ds(d * side, side)
        a = jnp.dot(x_ref[chunk, at, :], enc_ref[...], preferred_element_type=jnp.float32)
        b = jnp.dot(y_ref[chunk, at, :], dec_ref[...], preferred_element_type=jnp.float32)
        return a, b

    def rs_copy(d, s, q):
        at = pl.ds(q * piece, piece)
        return pltpu.make_async_remote_copy(
            src_ref=slots.at[d, s, at],
            dst_ref=slots.at[d, s + 1, at],
            send_sem=rs_send.at[d, s, q],
            recv_sem=rs_recv.at[d, s, q],
            device_id={"seq": nexts[d]},
            device_id_type=pl.DeviceIdType.MESH,
        )

    def ag_copy(d, s, q, first):
        at = pl.ds(d * side + q * piece, piece)
        owner = ring_index(signed(d, s), n)
        return pltpu.make_async_remote_copy(
            src_ref=mine.at[at] if first else out_ref.at[owner, at],
            dst_ref=out_ref.at[owner, at],
            send_sem=ag_send.at[d, s, q],
            recv_sem=ag_recv.at[d, s, q],
            device_id={"seq": nexts[d]},
            device_id_type=pl.DeviceIdType.MESH,
        )

    for d in range(2):
        a, b = own_term(d, 1)
        slots[d, 0, :, :share] = a.astype(BF16)
        slots[d, 0, :, share:] = b.astype(BF16)
        for q in range(PIECES):
            rs_copy(d, 0, q).start()

    def fill(s):
        for d in range(2):
            a, b = own_term(d, s + 2)
            term[d, :, :share] = a
            term[d, :, share:] = b

    def rs_step(s, carry):
        fill(s)
        for q in range(PIECES):
            at = pl.ds(q * piece, piece)
            for d in range(2):
                rs_copy(d, s, q).wait_recv()
                total = slots[d, s + 1, at, :].astype(F32) + term[d, at, :]
                slots[d, s + 1, at, :] = total.astype(BF16)
                rs_copy(d, s + 1, q).start()
        return carry

    lax.fori_loop(0, n - 2, rs_step, 0)
    fill(n - 2)
    for q in range(PIECES):
        at = pl.ds(q * piece, piece)
        for d in range(2):
            rs_copy(d, n - 2, q).wait_recv()
            rows = pl.ds(d * side + q * piece, piece)
            pre = slots[d, n - 1, at, :share].astype(F32) + term[d, at, :share]
            grad = slots[d, n - 1, at, share:].astype(F32) + term[d, at, share:]
            value, slope = gelu_and_slope(pre)
            mine[rows, :share] = value.astype(BF16)
            mine[rows, share:] = (grad * slope).astype(BF16)
            ag_copy(d, 0, q, True).start()
    local = pltpu.make_async_copy(mine, out_ref.at[me], local_sem)
    local.start()

    def ag_step(s, carry):
        for q in range(PIECES):
            for d in range(2):
                incoming(d, s, q).wait_recv()
                ag_copy(d, s + 1, q, False).start()
        return carry

    def incoming(d, s, q):
        at = pl.ds(d * side + q * piece, piece)
        owner = ring_index(signed(d, s + 1), n)
        return pltpu.make_async_remote_copy(
            src_ref=mine.at[at],
            dst_ref=out_ref.at[owner, at],
            send_sem=ag_send.at[d, s, q],
            recv_sem=ag_recv.at[d, s, q],
            device_id={"seq": nexts[d]},
            device_id_type=pl.DeviceIdType.MESH,
        )

    lax.fori_loop(0, n - 2, ag_step, 0)
    for q in range(PIECES):
        for d in range(2):
            incoming(d, n - 2, q).wait_recv()

    def drain(s, carry):
        for q in range(PIECES):
            for d in range(2):
                rs_copy(d, s, q).wait_send()
                ag_copy(d, s, q, True).wait_send()
        return carry

    lax.fori_loop(0, n - 1, drain, 0)
    local.wait()


def ring(pool_taps, cot_taps, enc_mat, dec_mat, n):
    half = pool_taps.shape[1]
    share = enc_mat.shape[1]
    depth = enc_mat.shape[0]
    vmem = pl.BlockSpec(memory_space=pltpu.VMEM)
    steps = (2, n - 1, PIECES)
    return pl.pallas_call(
        functools.partial(ring_kernel, n),
        out_shape=jax.ShapeDtypeStruct((n, half, 2 * share), BF16),
        in_specs=[vmem] * 4,
        out_specs=pl.BlockSpec(memory_space=pl.ANY),
        scratch_shapes=[
            pltpu.VMEM((2, n, half // 2, 2 * share), BF16),
            pltpu.VMEM((2, half // 2, 2 * share), F32),
            pltpu.VMEM((half, 2 * share), BF16),
            pltpu.SemaphoreType.DMA(steps),
            pltpu.SemaphoreType.DMA(steps),
            pltpu.SemaphoreType.DMA(steps),
            pltpu.SemaphoreType.DMA(steps),
            pltpu.SemaphoreType.DMA,
        ],
        compiler_params=pltpu.CompilerParams(
            collective_id=0, has_side_effects=True, vmem_limit_bytes=48 * 2**20
        ),
        cost_estimate=pl.CostEstimate(
            flops=4 * n * half * depth * share,
            bytes_accessed=4 * n * half * share * 2,
            transcendentals=half * share,
        ),
    )(pool_taps, cot_taps, enc_mat, dec_mat)


def wide_shards(inputs, enc_weight, dec_weight, cotangent):
    parts = lax.axis_size("seq")
    rows, width = inputs.shape
    half = rows // 2
    total = half * parts
    block, taps, share = enc_weight.shape
    half_width = cotangent.shape[1]

    pooled = (inputs.astype(F32).reshape(half, 2, width).sum(axis=1) * 0.5).astype(BF16)
    cot_full = lax.all_gather(cotangent, "chan", axis=1, tiled=True)
    core = lax.axis_index("chan")
    cores = lax.axis_size("chan")
    few = half // cores
    leaving = jnp.concatenate(
        [
            lax.dynamic_slice_in_dim(pooled, core * few, few, 0),
            lax.dynamic_slice_in_dim(cot_full, core * 2 * few, 2 * few, 0),
        ],
        axis=0,
    )
    columns = to_columns(leaving, parts).reshape(parts, 1, 3 * few, block)
    columns = lax.all_gather(columns, "chan", axis=1, tiled=True)
    pool_col = columns[:, :, :few].reshape(total, block)
    cot_col = columns[:, :, few:].reshape(total, 2, block).astype(F32)
    even = cot_col[:, 0]
    odd = cot_col[:, 1]
    pair = (even + odd).astype(BF16)
    cross = (odd + shift(even, 1)).astype(BF16)
    before = jnp.concatenate([even[:1].astype(BF16), cross[:-1]], axis=0)
    pool_taps = jnp.concatenate([shift(pool_col, t - 2) for t in range(taps)], axis=1)
    cot_taps = jnp.concatenate([shift(pair, 1), cross, pair, before, shift(pair, -1)], axis=1)
    enc_mat = enc_weight.transpose(1, 0, 2).reshape(taps * block, share)
    dec_mat = dec_weight.transpose(1, 0, 2).reshape(taps * block, share)

    joint = ring(
        pool_taps.reshape(parts, half, taps * block),
        cot_taps.reshape(parts, half, taps * block),
        enc_mat,
        dec_mat,
        parts,
    ).reshape(total, 2 * share)
    hidden_all = joint[:, :share]
    grad_all = joint[:, share:]

    contract_rows = (((0,), (0,)), ((), ()))
    contract_last = (((1,), (1,)), ((), ()))
    dec_grad = lax.dot_general(cot_taps, hidden_all, contract_rows, preferred_element_type=F32)
    enc_grad = lax.dot_general(pool_taps, grad_all, contract_rows, preferred_element_type=F32)
    dec_grad = dec_grad.astype(BF16).reshape(taps, block, share).transpose(1, 0, 2)
    enc_grad = enc_grad.astype(BF16).reshape(taps, block, share).transpose(1, 0, 2)

    dec_out = lax.dot_general(hidden_all, dec_mat, contract_last, preferred_element_type=F32)
    p0, p1, p2, p3, p4 = [dec_out[:, t * block : (t + 1) * block] for t in range(taps)]
    after4 = shift(p4, 1)
    before0 = shift(p0, -1)
    dec_even = before0 + shift(p1, -1) + p2 + p3 + after4
    dec_odd = before0 + p1 + p2 + shift(p3, 1) + after4
    decoded = jnp.stack([dec_even, dec_odd], axis=1).astype(BF16).reshape(parts, rows, block)
    enc_out = lax.dot_general(grad_all, enc_mat, contract_last, preferred_element_type=F32)
    pool_grad = sum(shift(enc_out[:, t * block : (t + 1) * block], 2 - t) for t in range(taps))
    pool_grad = pool_grad.astype(BF16).reshape(parts, half, block)
    mine = jnp.concatenate([decoded, pool_grad], axis=1)
    mine = lax.psum_scatter(mine, "chan", scatter_dimension=1, tiled=True)
    mine = lax.all_gather(to_rows(mine), "chan", axis=0, tiled=True)
    col_start = core * half_width
    mine = lax.dynamic_slice_in_dim(mine, col_start, half_width, 1).astype(F32)

    skip = lax.dynamic_slice_in_dim(inputs, col_start, half_width, 1)
    mixed_out = (skip.astype(F32) + mine[:rows]).astype(BF16)
    input_grad = (cotangent.astype(F32) + 0.5 * jnp.repeat(mine[rows:], 2, axis=0)).astype(BF16)
    return mixed_out, input_grad, enc_grad, dec_grad


PAD = 8
LANES = 128


def whole_kernel(
    n, own_ref, enc_ref, dec_ref, enc_grad_ref, dec_grad_ref, out_ref, gathered,
    both, padded, x_ref, y_ref, slots, term, mine, stage, acc, leaving, arriving,
    enc_sum, dec_sum, rs_send, rs_recv, ag_send, ag_recv, local_sem, stage_sem, pair_send, pair_recv,
):
    me = lax.axis_index("seq")
    core = lax.axis_index("chan")
    place = ring_place(me, n)
    nexts = (ring_index(place + 1, n), ring_index(place - 1, n))
    few, block = own_ref.shape[2:]
    half = 2 * few
    total = n * half
    share = enc_ref.shape[1]
    side = half // 2
    piece = side // PIECES
    mesh_ids = pl.DeviceIdType.MESH

    barrier = pltpu.get_barrier_semaphore()
    for other in nexts:
        pl.semaphore_signal(barrier, inc=1, device_id={"seq": other}, device_id_type=mesh_ids)
    pl.semaphore_signal(barrier, inc=1, device_id={"chan": 1 - core}, device_id_type=mesh_ids)
    pl.semaphore_wait(barrier, 3)

    def pair_copy(k, src, dst):
        return pltpu.make_async_remote_copy(
            src_ref=src,
            dst_ref=dst,
            send_sem=pair_send.at[k],
            recv_sem=pair_recv.at[k],
            device_id={"chan": 1 - core},
            device_id_type=mesh_ids,
        )

    swap = pair_copy(0, own_ref, both.at[core])
    swap.start()
    keep = pltpu.make_async_copy(own_ref, both.at[core], local_sem)
    keep.start()
    padded[...] = jnp.zeros_like(padded)
    x_ref[...] = jnp.zeros_like(x_ref)
    y_ref[...] = jnp.zeros_like(y_ref)
    acc[...] = jnp.zeros_like(acc)
    enc_sum[...] = jnp.zeros_like(enc_sum)
    dec_sum[...] = jnp.zeros_like(dec_sum)
    keep.wait()
    swap.wait()

    def widen(chunk, carry):
        for part in range(2):
            for k in range(3):
                at = pl.ds(pl.multiple_of(PAD + chunk * half + part * few, 8), few)
                padded[k, at, :block] = both[part, k, chunk].astype(F32)
        return carry

    lax.fori_loop(0, n, widen, 0)

    def taps_of(chunk, carry):
        def rows(k, by):
            return padded[k, pl.ds(chunk * half + (PAD + by), half), :block]

        for t in range(5):
            x_ref[chunk, :, t * LANES : t * LANES + block] = rows(0, t - 2).astype(BF16)
        for t, (a, b) in enumerate(((1, 1), (1, 0), (0, 0), (0, -1), (-1, -1))):
            both_rows = rows(1, a) + rows(2, b)
            y_ref[chunk, :, t * LANES : t * LANES + block] = both_rows.astype(BF16)
        return carry

    lax.fori_loop(0, n, taps_of, 0)

    def signed(d, steps):
        return place - steps if d == 0 else place + steps

    def own_term(d, steps):
        chunk = ring_index(signed(d, steps), n)
        at = pl.ds(d * side, side)
        a = jnp.dot(x_ref[chunk, at, :], enc_ref[...], preferred_element_type=F32)
        b = jnp.dot(y_ref[chunk, at, :], dec_ref[...], preferred_element_type=F32)
        return a, b

    def rs_copy(d, s, q):
        at = pl.ds(q * piece, piece)
        return pltpu.make_async_remote_copy(
            src_ref=slots.at[d, s, at],
            dst_ref=slots.at[d, s + 1, at],
            send_sem=rs_send.at[d, s, q],
            recv_sem=rs_recv.at[d, s, q],
            device_id={"seq": nexts[d]},
            device_id_type=mesh_ids,
        )

    def ag_copy(d, s, q, first, owner_steps):
        at = pl.ds(d * side + q * piece, piece)
        owner = ring_index(signed(d, owner_steps), n)
        return pltpu.make_async_remote_copy(
            src_ref=mine.at[at] if first else gathered.at[owner, at],
            dst_ref=gathered.at[owner, at],
            send_sem=ag_send.at[d, s, q],
            recv_sem=ag_recv.at[d, s, q],
            device_id={"seq": nexts[d]},
            device_id_type=mesh_ids,
        )

    for d in range(2):
        a, b = own_term(d, 1)
        slots[d, 0, :, :share] = a.astype(BF16)
        slots[d, 0, :, share:] = b.astype(BF16)
        for q in range(PIECES):
            rs_copy(d, 0, q).start()

    def fill(s):
        for d in range(2):
            a, b = own_term(d, s + 2)
            term[d, :, :share] = a
            term[d, :, share:] = b

    def rs_step(s, carry):
        fill(s)
        for q in range(PIECES):
            at = pl.ds(q * piece, piece)
            for d in range(2):
                rs_copy(d, s, q).wait_recv()
                summed = slots[d, s + 1, at, :].astype(F32) + term[d, at, :]
                slots[d, s + 1, at, :] = summed.astype(BF16)
                rs_copy(d, s + 1, q).start()
        return carry

    lax.fori_loop(0, n - 2, rs_step, 0)
    fill(n - 2)
    for q in range(PIECES):
        at = pl.ds(q * piece, piece)
        for d in range(2):
            rs_copy(d, n - 2, q).wait_recv()
            rows = pl.ds(d * side + q * piece, piece)
            pre = slots[d, n - 1, at, :share].astype(F32) + term[d, at, :share]
            grad = slots[d, n - 1, at, share:].astype(F32) + term[d, at, share:]
            value, slope = gelu_and_slope(pre)
            mine[rows, :share] = value.astype(BF16)
            mine[rows, share:] = (grad * slope).astype(BF16)
            ag_copy(d, 0, q, True, 0).start()

    contract_rows = (((0,), (0,)), ((), ()))
    contract_last = (((1,), (1,)), ((), ()))

    def consume(chunk, d, load):
        at = pl.ds(d * side, side)
        hid = load(slice(None, share))
        pre_grad = load(slice(share, None))
        dec_sum[...] += lax.dot_general(
            y_ref[chunk, at, :], hid, contract_rows, preferred_element_type=F32
        )
        enc_sum[...] += lax.dot_general(
            x_ref[chunk, at, :], pre_grad, contract_rows, preferred_element_type=F32
        )
        p = lax.dot_general(hid, dec_ref[...], contract_last, preferred_element_type=F32)
        g = lax.dot_general(pre_grad, enc_ref[...], contract_last, preferred_element_type=F32)
        p = [p[:, t * LANES : (t + 1) * LANES] for t in range(5)]
        base = chunk * half + (PAD + d * side)

        def add(k, by, what):
            to = pl.ds(base + by, side)
            acc[k, to, :] += what

        add(1, 1, p[0] + p[1])
        add(1, 0, p[2] + p[3])
        add(1, -1, p[4])
        add(2, 1, p[0])
        add(2, 0, p[1] + p[2])
        add(2, -1, p[3] + p[4])
        for t in range(5):
            add(0, t - 2, g[:, t * LANES : (t + 1) * LANES])

    for d in range(2):
        consume(me, d, lambda cols: mine[d * side : (d + 1) * side, cols])

    def stage_copy(d, s):
        owner = ring_index(signed(d, s + 1), n)
        return pltpu.make_async_copy(
            gathered.at[owner, pl.ds(d * side, side)], stage.at[d], stage_sem.at[d]
        )

    def take(s):
        for d in range(2):
            stage_copy(d, s).start()
        for d in range(2):
            stage_copy(d, s).wait()
            consume(ring_index(signed(d, s + 1), n), d, lambda cols: stage[d, :, cols])

    def ag_step(s, carry):
        for q in range(PIECES):
            for d in range(2):
                ag_copy(d, s, q, True, s + 1).wait_recv()
                ag_copy(d, s + 1, q, False, s + 1).start()
        take(s)
        return carry

    lax.fori_loop(0, n - 2, ag_step, 0)
    for q in range(PIECES):
        for d in range(2):
            ag_copy(d, n - 2, q, True, n - 1).wait_recv()
    take(n - 2)

    def pick(k, chunk, part):
        at = pl.ds(pl.multiple_of(PAD + chunk * half + part * few, 8), few)
        return acc[k, at, :block]

    def pack(chunk, carry):
        for k in range(3):
            leaving[k, chunk] = pick(k, chunk, 1 - core).astype(BF16)
        return carry

    lax.fori_loop(0, n, pack, 0)
    swap2 = pair_copy(1, leaving, arriving)
    swap2.start()
    enc_grad_ref[...] = enc_sum[...].astype(BF16)
    dec_grad_ref[...] = dec_sum[...].astype(BF16)

    def drain(s, carry):
        for q in range(PIECES):
            for d in range(2):
                rs_copy(d, s, q).wait_send()
                ag_copy(d, s, q, True, s).wait_send()
        return carry

    lax.fori_loop(0, n - 1, drain, 0)
    swap2.wait()

    def finish(chunk, carry):
        for k in range(3):
            summed = pick(k, chunk, core) + arriving[k, chunk].astype(F32)
            out_ref[chunk, k * few : (k + 1) * few, :] = summed.astype(BF16)
        return carry

    lax.fori_loop(0, n, finish, 0)


def whole_ring(own, enc_mat, dec_mat):
    n, few, block = own.shape[1:]
    half = 2 * few
    depth, share = enc_mat.shape
    vmem = pl.BlockSpec(memory_space=pltpu.VMEM)
    steps = (2, n - 1, PIECES)
    dma = pltpu.SemaphoreType.DMA
    return pl.pallas_call(
        functools.partial(whole_kernel, n),
        out_shape=[
            jax.ShapeDtypeStruct((depth, share), BF16),
            jax.ShapeDtypeStruct((depth, share), BF16),
            jax.ShapeDtypeStruct((n, 3 * few, block), BF16),
            jax.ShapeDtypeStruct((n, half, 2 * share), BF16),
        ],
        in_specs=[vmem] * 3,
        out_specs=[vmem] * 3 + [pl.BlockSpec(memory_space=pl.ANY)],
        scratch_shapes=[
            pltpu.VMEM((2,) + own.shape, BF16),
            pltpu.VMEM((3, n * half + 2 * PAD, LANES), F32),
            pltpu.VMEM((n, half, depth), BF16),
            pltpu.VMEM((n, half, depth), BF16),
            pltpu.VMEM((2, n, half // 2, 2 * share), BF16),
            pltpu.VMEM((2, half // 2, 2 * share), F32),
            pltpu.VMEM((half, 2 * share), BF16),
            pltpu.VMEM((2, half // 2, 2 * share), BF16),
            pltpu.VMEM((3, n * half + 2 * PAD, LANES), F32),
            pltpu.VMEM(own.shape, BF16),
            pltpu.VMEM(own.shape, BF16),
            pltpu.VMEM((depth, share), F32),
            pltpu.VMEM((depth, share), F32),
            dma(steps), dma(steps), dma(steps), dma(steps), dma, dma((2,)), dma((2,)), dma((2,)),
        ],
        compiler_params=pltpu.CompilerParams(
            collective_id=0, has_side_effects=True, vmem_limit_bytes=56 * 2**20
        ),
        cost_estimate=pl.CostEstimate(
            flops=12 * n * half * depth * share,
            bytes_accessed=8 * n * half * share,
            transcendentals=half * share,
        ),
    )(own, enc_mat, dec_mat)[:3]


def shards(inputs, enc_weight, dec_weight, cotangent):
    parts = lax.axis_size("seq")
    cores = lax.axis_size("chan")
    rows, width = inputs.shape
    half = rows // 2
    few = half // 2
    block, taps, share = enc_weight.shape
    half_width = cotangent.shape[1]
    if cores != 2 or taps != 5 or block > LANES or parts * half > 2048:
        return wide_shards(inputs, enc_weight, dec_weight, cotangent)
    core = lax.axis_index("chan")

    some = lax.dynamic_slice_in_dim(inputs, core * half, half, 0)
    pooled = (some.astype(F32).reshape(few, 2, width).sum(axis=1) * 0.5).astype(BF16)
    cot_full = lax.all_gather(cotangent, "chan", axis=1, tiled=True)
    cot_some = lax.dynamic_slice_in_dim(cot_full, core * half, half, 0).reshape(few, 2, width)
    leaving = jnp.concatenate([pooled, cot_some[:, 0], cot_some[:, 1]], axis=0)
    columns = to_columns(leaving, parts).reshape(parts, 3, few, block).transpose(1, 0, 2, 3)

    def matrix(weight):
        fill = ((0, 0), (0, LANES - block), (0, 0))
        return jnp.pad(weight.transpose(1, 0, 2), fill).reshape(taps * LANES, share)

    enc_grad, dec_grad, back = whole_ring(columns, matrix(enc_weight), matrix(dec_weight))

    def unfold(grad):
        return grad.reshape(taps, LANES, share)[:, :block].transpose(1, 0, 2)

    mine = lax.all_gather(to_rows(back), "chan", axis=0, tiled=False)
    col_start = core * half_width
    mine = lax.dynamic_slice_in_dim(mine, col_start, half_width, 2).astype(F32)
    mine = mine.reshape(2, 3, few, half_width)
    pool_grad = mine[:, 0].reshape(half, half_width)
    decoded = jnp.stack([mine[:, 1], mine[:, 2]], axis=2).reshape(rows, half_width)
    skip = lax.dynamic_slice_in_dim(inputs, col_start, half_width, 1)
    mixed_out = (skip.astype(F32) + decoded).astype(BF16)
    input_grad = (cotangent.astype(F32) + 0.5 * jnp.repeat(pool_grad, 2, axis=0)).astype(BF16)
    return mixed_out, input_grad, unfold(enc_grad), unfold(dec_grad)


def solution(mesh):
    return jax.shard_map(
        shards,
        mesh=mesh,
        in_specs=(
            P(("groups", "seq"), None),
            P("seq", None, "chan"),
            P("seq", None, "chan"),
            P(("groups", "seq"), "chan"),
        ),
        out_specs=(
            P(("groups", "seq"), "chan"),
            P(("groups", "seq"), "chan"),
            P(("groups", "seq"), None, "chan"),
            P(("groups", "seq"), None, "chan"),
        ),
        check_vma=False,
    )
```

```python
import functools
import math

import jax
import jax.numpy as jnp
from jax import lax
from jax.experimental import pallas as pl
from jax.experimental.pallas import tpu as pltpu
from jax.sharding import PartitionSpec as P

BF16 = jnp.bfloat16
F32 = jnp.float32


def shift(array, by):
    length = array.shape[0]
    if by == 0:
        return array
    pad = jnp.zeros((abs(by),) + array.shape[1:], array.dtype)
    if by > 0:
        return jnp.concatenate([array[by:], pad], axis=0)
    return jnp.concatenate([pad, array[: length + by]], axis=0)


def to_columns(array, parts):
    rows, cols = array.shape
    blocks = array.reshape(rows, parts, cols // parts).transpose(1, 0, 2)
    return lax.all_to_all(blocks, "seq", 0, 0, tiled=True)


def to_rows(blocks):
    parts, rows, cols = blocks.shape
    got = lax.all_to_all(blocks, "seq", 0, 0, tiled=True)
    return got.transpose(1, 0, 2).reshape(rows, parts * cols)


PIECES = 2


def ring_place(index, n):
    if n != 8:
        return index
    y = lax.rem(index, 2)
    z = index // 2
    return z + y * (n - 1 - 2 * z)


def ring_index(place, n):
    place = lax.rem(place + 2 * n, n)
    if n != 8:
        return place
    back = place // (n // 2)
    return 2 * place + back * (2 * n - 1 - 4 * place)


def gelu_and_slope(v):
    scale = math.sqrt(2.0 / math.pi)
    square = v * v
    th = jnp.tanh(scale * (v + 0.044715 * square * v))
    up = 0.5 * (1.0 + th)
    slope = up + 0.5 * v * (1.0 - th * th) * (scale * (1.0 + 3.0 * 0.044715 * square))
    return v * up, slope


def ring_kernel(
    n, x_ref, y_ref, enc_ref, dec_ref, out_ref, slots, term, mine,
    rs_send, rs_recv, ag_send, ag_recv, local_sem,
):
    me = lax.axis_index("seq")
    place = ring_place(me, n)
    nexts = (ring_index(place + 1, n), ring_index(place - 1, n))
    half = x_ref.shape[1]
    share = enc_ref.shape[1]
    side = half // 2
    piece = side // PIECES

    barrier = pltpu.get_barrier_semaphore()
    for other in nexts:
        pl.semaphore_signal(
            barrier, inc=1, device_id={"seq": other}, device_id_type=pl.DeviceIdType.MESH
        )
    pl.semaphore_wait(barrier, 2)

    def signed(d, steps):
        return place - steps if d == 0 else place + steps

    def own_term(d, steps):
        chunk = ring_index(signed(d, steps), n)
        at = pl.ds(d * side, side)
        a = jnp.dot(x_ref[chunk, at, :], enc_ref[...], preferred_element_type=jnp.float32)
        b = jnp.dot(y_ref[chunk, at, :], dec_ref[...], preferred_element_type=jnp.float32)
        return a, b

    def rs_copy(d, s, q):
        at = pl.ds(q * piece, piece)
        return pltpu.make_async_remote_copy(
            src_ref=slots.at[d, s, at],
            dst_ref=slots.at[d, s + 1, at],
            send_sem=rs_send.at[d, s, q],
            recv_sem=rs_recv.at[d, s, q],
            device_id={"seq": nexts[d]},
            device_id_type=pl.DeviceIdType.MESH,
        )

    def ag_copy(d, s, q, first):
        at = pl.ds(d * side + q * piece, piece)
        owner = ring_index(signed(d, s), n)
        return pltpu.make_async_remote_copy(
            src_ref=mine.at[at] if first else out_ref.at[owner, at],
            dst_ref=out_ref.at[owner, at],
            send_sem=ag_send.at[d, s, q],
            recv_sem=ag_recv.at[d, s, q],
            device_id={"seq": nexts[d]},
            device_id_type=pl.DeviceIdType.MESH,
        )

    for d in range(2):
        a, b = own_term(d, 1)
        slots[d, 0, :, :share] = a.astype(BF16)
        slots[d, 0, :, share:] = b.astype(BF16)
        for q in range(PIECES):
            rs_copy(d, 0, q).start()

    def fill(s):
        for d in range(2):
            a, b = own_term(d, s + 2)
            term[d, :, :share] = a
            term[d, :, share:] = b

    def rs_step(s, carry):
        fill(s)
        for q in range(PIECES):
            at = pl.ds(q * piece, piece)
            for d in range(2):
                rs_copy(d, s, q).wait_recv()
                total = slots[d, s + 1, at, :].astype(F32) + term[d, at, :]
                slots[d, s + 1, at, :] = total.astype(BF16)
                rs_copy(d, s + 1, q).start()
        return carry

    lax.fori_loop(0, n - 2, rs_step, 0)
    fill(n - 2)
    for q in range(PIECES):
        at = pl.ds(q * piece, piece)
        for d in range(2):
            rs_copy(d, n - 2, q).wait_recv()
            rows = pl.ds(d * side + q * piece, piece)
            pre = slots[d, n - 1, at, :share].astype(F32) + term[d, at, :share]
            grad = slots[d, n - 1, at, share:].astype(F32) + term[d, at, share:]
            value, slope = gelu_and_slope(pre)
            mine[rows, :share] = value.astype(BF16)
            mine[rows, share:] = (grad * slope).astype(BF16)
            ag_copy(d, 0, q, True).start()
    local = pltpu.make_async_copy(mine, out_ref.at[me], local_sem)
    local.start()

    def ag_step(s, carry):
        for q in range(PIECES):
            for d in range(2):
                incoming(d, s, q).wait_recv()
                ag_copy(d, s + 1, q, False).start()
        return carry

    def incoming(d, s, q):
        at = pl.ds(d * side + q * piece, piece)
        owner = ring_index(signed(d, s + 1), n)
        return pltpu.make_async_remote_copy(
            src_ref=mine.at[at],
            dst_ref=out_ref.at[owner, at],
            send_sem=ag_send.at[d, s, q],
            recv_sem=ag_recv.at[d, s, q],
            device_id={"seq": nexts[d]},
            device_id_type=pl.DeviceIdType.MESH,
        )

    lax.fori_loop(0, n - 2, ag_step, 0)
    for q in range(PIECES):
        for d in range(2):
            incoming(d, n - 2, q).wait_recv()

    def drain(s, carry):
        for q in range(PIECES):
            for d in range(2):
                rs_copy(d, s, q).wait_send()
                ag_copy(d, s, q, True).wait_send()
        return carry

    lax.fori_loop(0, n - 1, drain, 0)
    local.wait()


def ring(pool_taps, cot_taps, enc_mat, dec_mat, n):
    half = pool_taps.shape[1]
    share = enc_mat.shape[1]
    depth = enc_mat.shape[0]
    vmem = pl.BlockSpec(memory_space=pltpu.VMEM)
    steps = (2, n - 1, PIECES)
    return pl.pallas_call(
        functools.partial(ring_kernel, n),
        out_shape=jax.ShapeDtypeStruct((n, half, 2 * share), BF16),
        in_specs=[vmem] * 4,
        out_specs=pl.BlockSpec(memory_space=pl.ANY),
        scratch_shapes=[
            pltpu.VMEM((2, n, half // 2, 2 * share), BF16),
            pltpu.VMEM((2, half // 2, 2 * share), F32),
            pltpu.VMEM((half, 2 * share), BF16),
            pltpu.SemaphoreType.DMA(steps),
            pltpu.SemaphoreType.DMA(steps),
            pltpu.SemaphoreType.DMA(steps),
            pltpu.SemaphoreType.DMA(steps),
            pltpu.SemaphoreType.DMA,
        ],
        compiler_params=pltpu.CompilerParams(
            collective_id=0, has_side_effects=True, vmem_limit_bytes=48 * 2**20
        ),
        cost_estimate=pl.CostEstimate(
            flops=4 * n * half * depth * share,
            bytes_accessed=4 * n * half * share * 2,
            transcendentals=half * share,
        ),
    )(pool_taps, cot_taps, enc_mat, dec_mat)


def wide_shards(inputs, enc_weight, dec_weight, cotangent):
    parts = lax.axis_size("seq")
    rows, width = inputs.shape
    half = rows // 2
    total = half * parts
    block, taps, share = enc_weight.shape
    half_width = cotangent.shape[1]

    pooled = (inputs.astype(F32).reshape(half, 2, width).sum(axis=1) * 0.5).astype(BF16)
    cot_full = lax.all_gather(cotangent, "chan", axis=1, tiled=True)
    core = lax.axis_index("chan")
    cores = lax.axis_size("chan")
    few = half // cores
    leaving = jnp.concatenate(
        [
            lax.dynamic_slice_in_dim(pooled, core * few, few, 0),
            lax.dynamic_slice_in_dim(cot_full, core * 2 * few, 2 * few, 0),
        ],
        axis=0,
    )
    columns = to_columns(leaving, parts).reshape(parts, 1, 3 * few, block)
    columns = lax.all_gather(columns, "chan", axis=1, tiled=True)
    pool_col = columns[:, :, :few].reshape(total, block)
    cot_col = columns[:, :, few:].reshape(total, 2, block).astype(F32)
    even = cot_col[:, 0]
    odd = cot_col[:, 1]
    pair = (even + odd).astype(BF16)
    cross = (odd + shift(even, 1)).astype(BF16)
    before = jnp.concatenate([even[:1].astype(BF16), cross[:-1]], axis=0)
    pool_taps = jnp.concatenate([shift(pool_col, t - 2) for t in range(taps)], axis=1)
    cot_taps = jnp.concatenate([shift(pair, 1), cross, pair, before, shift(pair, -1)], axis=1)
    enc_mat = enc_weight.transpose(1, 0, 2).reshape(taps * block, share)
    dec_mat = dec_weight.transpose(1, 0, 2).reshape(taps * block, share)

    joint = ring(
        pool_taps.reshape(parts, half, taps * block),
        cot_taps.reshape(parts, half, taps * block),
        enc_mat,
        dec_mat,
        parts,
    ).reshape(total, 2 * share)
    hidden_all = joint[:, :share]
    grad_all = joint[:, share:]

    contract_rows = (((0,), (0,)), ((), ()))
    contract_last = (((1,), (1,)), ((), ()))
    dec_grad = lax.dot_general(cot_taps, hidden_all, contract_rows, preferred_element_type=F32)
    enc_grad = lax.dot_general(pool_taps, grad_all, contract_rows, preferred_element_type=F32)
    dec_grad = dec_grad.astype(BF16).reshape(taps, block, share).transpose(1, 0, 2)
    enc_grad = enc_grad.astype(BF16).reshape(taps, block, share).transpose(1, 0, 2)

    dec_out = lax.dot_general(hidden_all, dec_mat, contract_last, preferred_element_type=F32)
    p0, p1, p2, p3, p4 = [dec_out[:, t * block : (t + 1) * block] for t in range(taps)]
    after4 = shift(p4, 1)
    before0 = shift(p0, -1)
    dec_even = before0 + shift(p1, -1) + p2 + p3 + after4
    dec_odd = before0 + p1 + p2 + shift(p3, 1) + after4
    decoded = jnp.stack([dec_even, dec_odd], axis=1).astype(BF16).reshape(parts, rows, block)
    enc_out = lax.dot_general(grad_all, enc_mat, contract_last, preferred_element_type=F32)
    pool_grad = sum(shift(enc_out[:, t * block : (t + 1) * block], 2 - t) for t in range(taps))
    pool_grad = pool_grad.astype(BF16).reshape(parts, half, block)
    mine = jnp.concatenate([decoded, pool_grad], axis=1)
    mine = lax.psum_scatter(mine, "chan", scatter_dimension=1, tiled=True)
    mine = lax.all_gather(to_rows(mine), "chan", axis=0, tiled=True)
    col_start = core * half_width
    mine = lax.dynamic_slice_in_dim(mine, col_start, half_width, 1).astype(F32)

    skip = lax.dynamic_slice_in_dim(inputs, col_start, half_width, 1)
    mixed_out = (skip.astype(F32) + mine[:rows]).astype(BF16)
    input_grad = (cotangent.astype(F32) + 0.5 * jnp.repeat(mine[rows:], 2, axis=0)).astype(BF16)
    return mixed_out, input_grad, enc_grad, dec_grad


PAD = 8
LANES = 128


def whole_kernel(
    n, own_ref, enc_ref, dec_ref, enc_grad_ref, dec_grad_ref, out_ref, gathered,
    both, padded, x_ref, y_ref, slots, term, mine, stage, acc, leaving, arriving, settled, landed,
    enc_sum, dec_sum, rs_send, rs_recv, ag_send, ag_recv, local_sem, stage_sem,
    out_send, out_recv, pair_send, pair_recv, back_send, back_recv, sum_send, sum_recv, last_send, last_recv,
):
    me = lax.axis_index("seq")
    core = lax.axis_index("chan")
    place = ring_place(me, n)
    nexts = (ring_index(place + 1, n), ring_index(place - 1, n))
    few, block = own_ref.shape[1] // 3, own_ref.shape[2]
    half = 2 * few
    share = enc_ref.shape[1]
    side = half // 2
    piece = side // PIECES
    mesh_ids = pl.DeviceIdType.MESH

    barrier = pltpu.get_barrier_semaphore()
    around = [i if up else -i for i in range(1, n // 2 + 1) for up in (True, False)][: n - 1]
    others = [ring_index(place + i, n) for i in around]
    sources = [ring_index(place - i, n) for i in around]
    for other in others:
        pl.semaphore_signal(barrier, inc=1, device_id={"seq": other}, device_id_type=mesh_ids)
    pl.semaphore_signal(barrier, inc=1, device_id={"chan": 1 - core}, device_id_type=mesh_ids)
    pl.semaphore_wait(barrier, n)

    def remote(src, dst, send, recv, where):
        return pltpu.make_async_remote_copy(
            src_ref=src,
            dst_ref=dst,
            send_sem=send,
            recv_sem=recv,
            device_id=where,
            device_id_type=mesh_ids,
        )

    other_core = {"chan": 1 - core}

    def out_copy(i):
        return remote(
            own_ref.at[others[i]], both.at[core, me], out_send.at[i], out_recv.at[i], {"seq": others[i]}
        )

    def pair_copy(i, chunk, part):
        block_of = both.at[part, chunk]
        return remote(block_of, block_of, pair_send.at[i], pair_recv.at[i], other_core)

    for i in range(n - 1):
        out_copy(i).start()
    keep = pltpu.make_async_copy(own_ref.at[me], both.at[core, me], local_sem)
    keep.start()
    padded[...] = jnp.zeros_like(padded)
    x_ref[...] = jnp.zeros_like(x_ref)
    y_ref[...] = jnp.zeros_like(y_ref)
    acc[...] = jnp.zeros_like(acc)
    enc_sum[...] = jnp.zeros_like(enc_sum)
    dec_sum[...] = jnp.zeros_like(dec_sum)
    keep.wait()
    pair_copy(n - 1, me, core).start()
    for i in range(n - 1):
        remote(
            own_ref.at[me], both.at[core, sources[i]], out_send.at[i], out_recv.at[i], {"seq": others[i]}
        ).wait_recv()
        pair_copy(i, sources[i], core).start()
    pair_copy(n - 1, me, 1 - core).wait_recv()
    for i in range(n - 1):
        pair_copy(i, sources[i], 1 - core).wait_recv()

    def widen(chunk, carry):
        for part in range(2):
            for k in range(3):
                at = pl.ds(pl.multiple_of(PAD + chunk * half + part * few, 8), few)
                padded[k, at, :block] = both[part, chunk, k * few : (k + 1) * few].astype(F32)
        return carry

    lax.fori_loop(0, n, widen, 0)

    def taps_of(chunk, carry):
        def rows(k, by):
            return padded[k, pl.ds(chunk * half + (PAD + by), half), :block]

        for t in range(5):
            x_ref[chunk, :, t * LANES : t * LANES + block] = rows(0, t - 2).astype(BF16)
        for t, (a, b) in enumerate(((1, 1), (1, 0), (0, 0), (0, -1), (-1, -1))):
            both_rows = rows(1, a) + rows(2, b)
            y_ref[chunk, :, t * LANES : t * LANES + block] = both_rows.astype(BF16)
        return carry

    lax.fori_loop(0, n, taps_of, 0)

    def signed(d, steps):
        return place - steps if d == 0 else place + steps

    def own_term(d, steps):
        chunk = ring_index(signed(d, steps), n)
        at = pl.ds(d * side, side)
        a = jnp.dot(x_ref[chunk, at, :], enc_ref[...], preferred_element_type=F32)
        b = jnp.dot(y_ref[chunk, at, :], dec_ref[...], preferred_element_type=F32)
        return a, b

    def rs_copy(d, s, q):
        at = pl.ds(q * piece, piece)
        return pltpu.make_async_remote_copy(
            src_ref=slots.at[d, s, at],
            dst_ref=slots.at[d, s + 1, at],
            send_sem=rs_send.at[d, s, q],
            recv_sem=rs_recv.at[d, s, q],
            device_id={"seq": nexts[d]},
            device_id_type=mesh_ids,
        )

    def ag_copy(d, s, q, first, owner_steps):
        at = pl.ds(d * side + q * piece, piece)
        owner = ring_index(signed(d, owner_steps), n)
        return pltpu.make_async_remote_copy(
            src_ref=mine.at[at] if first else gathered.at[owner, at],
            dst_ref=gathered.at[owner, at],
            send_sem=ag_send.at[d, s, q],
            recv_sem=ag_recv.at[d, s, q],
            device_id={"seq": nexts[d]},
            device_id_type=mesh_ids,
        )

    for d in range(2):
        a, b = own_term(d, 1)
        slots[d, 0, :, :share] = a.astype(BF16)
        slots[d, 0, :, share:] = b.astype(BF16)
        for q in range(PIECES):
            rs_copy(d, 0, q).start()

    def fill(s):
        for d in range(2):
            a, b = own_term(d, s + 2)
            term[d, :, :share] = a
            term[d, :, share:] = b

    def rs_step(s, carry):
        fill(s)
        for q in range(PIECES):
            at = pl.ds(q * piece, piece)
            for d in range(2):
                rs_copy(d, s, q).wait_recv()
                summed = slots[d, s + 1, at, :].astype(F32) + term[d, at, :]
                slots[d, s + 1, at, :] = summed.astype(BF16)
                rs_copy(d, s + 1, q).start()
        return carry

    lax.fori_loop(0, n - 2, rs_step, 0)
    fill(n - 2)
    for q in range(PIECES):
        at = pl.ds(q * piece, piece)
        for d in range(2):
            rs_copy(d, n - 2, q).wait_recv()
            rows = pl.ds(d * side + q * piece, piece)
            pre = slots[d, n - 1, at, :share].astype(F32) + term[d, at, :share]
            grad = slots[d, n - 1, at, share:].astype(F32) + term[d, at, share:]
            value, slope = gelu_and_slope(pre)
            mine[rows, :share] = value.astype(BF16)
            mine[rows, share:] = (grad * slope).astype(BF16)
            ag_copy(d, 0, q, True, 0).start()

    contract_rows = (((0,), (0,)), ((), ()))
    contract_last = (((1,), (1,)), ((), ()))

    def consume(chunk, d, load):
        at = pl.ds(d * side, side)
        hid = load(slice(None, share))
        pre_grad = load(slice(share, None))
        dec_sum[...] += lax.dot_general(
            y_ref[chunk, at, :], hid, contract_rows, preferred_element_type=F32
        )
        enc_sum[...] += lax.dot_general(
            x_ref[chunk, at, :], pre_grad, contract_rows, preferred_element_type=F32
        )
        p = lax.dot_general(hid, dec_ref[...], contract_last, preferred_element_type=F32)
        g = lax.dot_general(pre_grad, enc_ref[...], contract_last, preferred_element_type=F32)
        p = [p[:, t * LANES : (t + 1) * LANES] for t in range(5)]
        base = chunk * half + (PAD + d * side)

        def add(k, by, what):
            to = pl.ds(base + by, side)
            acc[k, to, :] += what

        add(1, 1, p[0] + p[1])
        add(1, 0, p[2] + p[3])
        add(1, -1, p[4])
        add(2, 1, p[0])
        add(2, 0, p[1] + p[2])
        add(2, -1, p[3] + p[4])
        for t in range(5):
            add(0, t - 2, g[:, t * LANES : (t + 1) * LANES])

    for d in range(2):
        consume(me, d, lambda cols: mine[d * side : (d + 1) * side, cols])

    def stage_copy(d, s):
        owner = ring_index(signed(d, s + 1), n)
        return pltpu.make_async_copy(
            gathered.at[owner, pl.ds(d * side, side)], stage.at[d], stage_sem.at[d]
        )

    def take(s):
        for d in range(2):
            stage_copy(d, s).start()
        for d in range(2):
            stage_copy(d, s).wait()
            consume(ring_index(signed(d, s + 1), n), d, lambda cols: stage[d, :, cols])

    def ag_step(s, carry):
        for q in range(PIECES):
            for d in range(2):
                ag_copy(d, s, q, True, s + 1).wait_recv()
                ag_copy(d, s + 1, q, False, s + 1).start()
        take(s)
        return carry

    lax.fori_loop(0, n - 2, ag_step, 0)
    for q in range(PIECES):
        for d in range(2):
            ag_copy(d, n - 2, q, True, n - 1).wait_recv()
    take(n - 2)

    def pick(k, chunk, part):
        at = pl.ds(pl.multiple_of(PAD + chunk * half + part * few, 8), few)
        return acc[k, at, :block]

    def sum_copy(i, chunk):
        return remote(leaving.at[chunk], arriving.at[chunk], sum_send.at[i], sum_recv.at[i], other_core)

    def back_copy(i, to, at):
        return remote(settled.at[to], landed.at[at], back_send.at[i], back_recv.at[i], {"seq": others[i]})

    order = others + [me]
    for i in range(n):
        for k in range(3):
            leaving[order[i], k * few : (k + 1) * few] = pick(k, order[i], 1 - core).astype(BF16)
        sum_copy(i, order[i]).start()
    for i in range(n):
        chunk = order[i]
        sum_copy(i, chunk).wait_recv()
        for k in range(3):
            at = slice(k * few, (k + 1) * few)
            summed = pick(k, chunk, core) + arriving[chunk, at].astype(F32)
            settled[chunk, at] = summed.astype(BF16)
        if i < n - 1:
            back_copy(i, chunk, me).start()
    keep_back = pltpu.make_async_copy(settled.at[me], landed.at[me], local_sem)
    keep_back.start()
    enc_grad_ref[...] = enc_sum[...].astype(BF16)
    dec_grad_ref[...] = dec_sum[...].astype(BF16)

    def drain(s, carry):
        for q in range(PIECES):
            for d in range(2):
                rs_copy(d, s, q).wait_send()
                ag_copy(d, s, q, True, s).wait_send()
        return carry

    lax.fori_loop(0, n - 1, drain, 0)
    for i in range(n):
        pair_copy(i, me, core).wait_send()
        sum_copy(i, me).wait_send()
    for i in range(n - 1):
        out_copy(i).wait_send()
    keep_back.wait()
    for i in range(n - 1):
        back_copy(i, me, sources[i]).wait_recv()
    theirs = landed.at[pl.ds((1 - core) * (n // 2), n // 2)]
    last = remote(theirs, out_ref.at[core], last_send, last_recv, other_core)
    last.start()
    ours = pltpu.make_async_copy(
        landed.at[pl.ds(core * (n // 2), n // 2)], out_ref.at[core], local_sem
    )
    ours.start()
    for i in range(n - 1):
        back_copy(i, me, me).wait_send()
    ours.wait()
    last.wait()


def whole_ring(own, enc_mat, dec_mat):
    n, triple, block = own.shape
    half = triple // 3 * 2
    depth, share = enc_mat.shape
    vmem = pl.BlockSpec(memory_space=pltpu.VMEM)
    steps = (2, n - 1, PIECES)
    dma = pltpu.SemaphoreType.DMA
    return pl.pallas_call(
        functools.partial(whole_kernel, n),
        out_shape=[
            jax.ShapeDtypeStruct((depth, share), BF16),
            jax.ShapeDtypeStruct((depth, share), BF16),
            jax.ShapeDtypeStruct((2, n // 2, triple, block), BF16),
            jax.ShapeDtypeStruct((n, half, 2 * share), BF16),
        ],
        in_specs=[vmem] * 3,
        out_specs=[vmem] * 3 + [pl.BlockSpec(memory_space=pl.ANY)],
        scratch_shapes=[
            pltpu.VMEM((2,) + own.shape, BF16),
            pltpu.VMEM((3, n * half + 2 * PAD, LANES), F32),
            pltpu.VMEM((n, half, depth), BF16),
            pltpu.VMEM((n, half, depth), BF16),
            pltpu.VMEM((2, n, half // 2, 2 * share), BF16),
            pltpu.VMEM((2, half // 2, 2 * share), F32),
            pltpu.VMEM((half, 2 * share), BF16),
            pltpu.VMEM((2, half // 2, 2 * share), BF16),
            pltpu.VMEM((3, n * half + 2 * PAD, LANES), F32),
            pltpu.VMEM(own.shape, BF16),
            pltpu.VMEM(own.shape, BF16),
            pltpu.VMEM(own.shape, BF16),
            pltpu.VMEM(own.shape, BF16),
            pltpu.VMEM((depth, share), F32),
            pltpu.VMEM((depth, share), F32),
            dma(steps), dma(steps), dma(steps), dma(steps), dma, dma((2,)),
            dma((n,)), dma((n,)), dma((n,)), dma((n,)), dma((n,)), dma((n,)), dma((n,)), dma((n,)), dma, dma,
        ],
        compiler_params=pltpu.CompilerParams(
            collective_id=0, has_side_effects=True, vmem_limit_bytes=56 * 2**20
        ),
        cost_estimate=pl.CostEstimate(
            flops=12 * n * half * depth * share,
            bytes_accessed=8 * n * half * share,
            transcendentals=half * share,
        ),
    )(own, enc_mat, dec_mat)[:3]


def shards(inputs, enc_weight, dec_weight, cotangent):
    parts = lax.axis_size("seq")
    cores = lax.axis_size("chan")
    rows, width = inputs.shape
    half = rows // 2
    few = half // 2
    block, taps, share = enc_weight.shape
    half_width = cotangent.shape[1]
    if cores != 2 or taps != 5 or block > LANES or parts * half > 2048 or parts % 2:
        return wide_shards(inputs, enc_weight, dec_weight, cotangent)
    core = lax.axis_index("chan")

    some = lax.dynamic_slice_in_dim(inputs, core * half, half, 0)
    pooled = (some.astype(F32).reshape(few, 2, width).sum(axis=1) * 0.5).astype(BF16)
    cot_full = lax.all_gather(cotangent, "chan", axis=1, tiled=True)
    cot_some = lax.dynamic_slice_in_dim(cot_full, core * half, half, 0).reshape(few, 2, width)
    leaving = jnp.concatenate([pooled, cot_some[:, 0], cot_some[:, 1]], axis=0)
    columns = leaving.reshape(3 * few, parts, block).transpose(1, 0, 2)

    def matrix(weight):
        fill = ((0, 0), (0, LANES - block), (0, 0))
        return jnp.pad(weight.transpose(1, 0, 2), fill).reshape(taps * LANES, share)

    enc_grad, dec_grad, back = whole_ring(columns, matrix(enc_weight), matrix(dec_weight))

    def unfold(grad):
        return grad.reshape(taps, LANES, share)[:, :block].transpose(1, 0, 2)

    col_start = core * half_width
    mine = back.astype(F32).transpose(0, 2, 1, 3).reshape(2, 3, few, half_width)
    pool_grad = mine[:, 0].reshape(half, half_width)
    decoded = jnp.stack([mine[:, 1], mine[:, 2]], axis=2).reshape(rows, half_width)
    skip = lax.dynamic_slice_in_dim(inputs, col_start, half_width, 1)
    mixed_out = (skip.astype(F32) + decoded).astype(BF16)
    input_grad = (cotangent.astype(F32) + 0.5 * jnp.repeat(pool_grad, 2, axis=0)).astype(BF16)
    return mixed_out, input_grad, unfold(enc_grad), unfold(dec_grad)


def solution(mesh):
    return jax.shard_map(
        shards,
        mesh=mesh,
        in_specs=(
            P(("groups", "seq"), None),
            P("seq", None, "chan"),
            P("seq", None, "chan"),
            P(("groups", "seq"), "chan"),
        ),
        out_specs=(
            P(("groups", "seq"), "chan"),
            P(("groups", "seq"), "chan"),
            P(("groups", "seq"), None, "chan"),
            P(("groups", "seq"), None, "chan"),
        ),
        check_vma=False,
    )
```

```python
import functools
import math

import jax
import jax.numpy as jnp
from jax import lax
from jax.experimental import pallas as pl
from jax.experimental.pallas import tpu as pltpu
from jax.sharding import PartitionSpec as P

BF16 = jnp.bfloat16
F32 = jnp.float32


def shift(array, by):
    length = array.shape[0]
    if by == 0:
        return array
    pad = jnp.zeros((abs(by),) + array.shape[1:], array.dtype)
    if by > 0:
        return jnp.concatenate([array[by:], pad], axis=0)
    return jnp.concatenate([pad, array[: length + by]], axis=0)


def to_columns(array, parts):
    rows, cols = array.shape
    blocks = array.reshape(rows, parts, cols // parts).transpose(1, 0, 2)
    return lax.all_to_all(blocks, "seq", 0, 0, tiled=True)


def to_rows(blocks):
    parts, rows, cols = blocks.shape
    got = lax.all_to_all(blocks, "seq", 0, 0, tiled=True)
    return got.transpose(1, 0, 2).reshape(rows, parts * cols)


PIECES = 2


def ring_place(index, n):
    if n != 8:
        return index
    y = lax.rem(index, 2)
    z = index // 2
    return z + y * (n - 1 - 2 * z)


def ring_index(place, n):
    place = lax.rem(place + 2 * n, n)
    if n != 8:
        return place
    back = place // (n // 2)
    return 2 * place + back * (2 * n - 1 - 4 * place)


def gelu_and_slope(v):
    scale = math.sqrt(2.0 / math.pi)
    square = v * v
    th = jnp.tanh(scale * (v + 0.044715 * square * v))
    up = 0.5 * (1.0 + th)
    slope = up + 0.5 * v * (1.0 - th * th) * (scale * (1.0 + 3.0 * 0.044715 * square))
    return v * up, slope


def ring_kernel(
    n, x_ref, y_ref, enc_ref, dec_ref, out_ref, slots, term, mine,
    rs_send, rs_recv, ag_send, ag_recv, local_sem,
):
    me = lax.axis_index("seq")
    place = ring_place(me, n)
    nexts = (ring_index(place + 1, n), ring_index(place - 1, n))
    half = x_ref.shape[1]
    share = enc_ref.shape[1]
    side = half // 2
    piece = side // PIECES

    barrier = pltpu.get_barrier_semaphore()
    for other in nexts:
        pl.semaphore_signal(
            barrier, inc=1, device_id={"seq": other}, device_id_type=pl.DeviceIdType.MESH
        )
    pl.semaphore_wait(barrier, 2)

    def signed(d, steps):
        return place - steps if d == 0 else place + steps

    def own_term(d, steps):
        chunk = ring_index(signed(d, steps), n)
        at = pl.ds(d * side, side)
        a = jnp.dot(x_ref[chunk, at, :], enc_ref[...], preferred_element_type=jnp.float32)
        b = jnp.dot(y_ref[chunk, at, :], dec_ref[...], preferred_element_type=jnp.float32)
        return a, b

    def rs_copy(d, s, q):
        at = pl.ds(q * piece, piece)
        return pltpu.make_async_remote_copy(
            src_ref=slots.at[d, s, at],
            dst_ref=slots.at[d, s + 1, at],
            send_sem=rs_send.at[d, s, q],
            recv_sem=rs_recv.at[d, s, q],
            device_id={"seq": nexts[d]},
            device_id_type=pl.DeviceIdType.MESH,
        )

    def ag_copy(d, s, q, first):
        at = pl.ds(d * side + q * piece, piece)
        owner = ring_index(signed(d, s), n)
        return pltpu.make_async_remote_copy(
            src_ref=mine.at[at] if first else out_ref.at[owner, at],
            dst_ref=out_ref.at[owner, at],
            send_sem=ag_send.at[d, s, q],
            recv_sem=ag_recv.at[d, s, q],
            device_id={"seq": nexts[d]},
            device_id_type=pl.DeviceIdType.MESH,
        )

    for d in range(2):
        a, b = own_term(d, 1)
        slots[d, 0, :, :share] = a.astype(BF16)
        slots[d, 0, :, share:] = b.astype(BF16)
        for q in range(PIECES):
            rs_copy(d, 0, q).start()

    def fill(s):
        for d in range(2):
            a, b = own_term(d, s + 2)
            term[d, :, :share] = a
            term[d, :, share:] = b

    def rs_step(s, carry):
        fill(s)
        for q in range(PIECES):
            at = pl.ds(q * piece, piece)
            for d in range(2):
                rs_copy(d, s, q).wait_recv()
                total = slots[d, s + 1, at, :].astype(F32) + term[d, at, :]
                slots[d, s + 1, at, :] = total.astype(BF16)
                rs_copy(d, s + 1, q).start()
        return carry

    lax.fori_loop(0, n - 2, rs_step, 0)
    fill(n - 2)
    for q in range(PIECES):
        at = pl.ds(q * piece, piece)
        for d in range(2):
            rs_copy(d, n - 2, q).wait_recv()
            rows = pl.ds(d * side + q * piece, piece)
            pre = slots[d, n - 1, at, :share].astype(F32) + term[d, at, :share]
            grad = slots[d, n - 1, at, share:].astype(F32) + term[d, at, share:]
            value, slope = gelu_and_slope(pre)
            mine[rows, :share] = value.astype(BF16)
            mine[rows, share:] = (grad * slope).astype(BF16)
            ag_copy(d, 0, q, True).start()
    local = pltpu.make_async_copy(mine, out_ref.at[me], local_sem)
    local.start()

    def ag_step(s, carry):
        for q in range(PIECES):
            for d in range(2):
                incoming(d, s, q).wait_recv()
                ag_copy(d, s + 1, q, False).start()
        return carry

    def incoming(d, s, q):
        at = pl.ds(d * side + q * piece, piece)
        owner = ring_index(signed(d, s + 1), n)
        return pltpu.make_async_remote_copy(
            src_ref=mine.at[at],
            dst_ref=out_ref.at[owner, at],
            send_sem=ag_send.at[d, s, q],
            recv_sem=ag_recv.at[d, s, q],
            device_id={"seq": nexts[d]},
            device_id_type=pl.DeviceIdType.MESH,
        )

    lax.fori_loop(0, n - 2, ag_step, 0)
    for q in range(PIECES):
        for d in range(2):
            incoming(d, n - 2, q).wait_recv()

    def drain(s, carry):
        for q in range(PIECES):
            for d in range(2):
                rs_copy(d, s, q).wait_send()
                ag_copy(d, s, q, True).wait_send()
        return carry

    lax.fori_loop(0, n - 1, drain, 0)
    local.wait()


def ring(pool_taps, cot_taps, enc_mat, dec_mat, n):
    half = pool_taps.shape[1]
    share = enc_mat.shape[1]
    depth = enc_mat.shape[0]
    vmem = pl.BlockSpec(memory_space=pltpu.VMEM)
    steps = (2, n - 1, PIECES)
    return pl.pallas_call(
        functools.partial(ring_kernel, n),
        out_shape=jax.ShapeDtypeStruct((n, half, 2 * share), BF16),
        in_specs=[vmem] * 4,
        out_specs=pl.BlockSpec(memory_space=pl.ANY),
        scratch_shapes=[
            pltpu.VMEM((2, n, half // 2, 2 * share), BF16),
            pltpu.VMEM((2, half // 2, 2 * share), F32),
            pltpu.VMEM((half, 2 * share), BF16),
            pltpu.SemaphoreType.DMA(steps),
            pltpu.SemaphoreType.DMA(steps),
            pltpu.SemaphoreType.DMA(steps),
            pltpu.SemaphoreType.DMA(steps),
            pltpu.SemaphoreType.DMA,
        ],
        compiler_params=pltpu.CompilerParams(
            collective_id=0, has_side_effects=True, vmem_limit_bytes=48 * 2**20
        ),
        cost_estimate=pl.CostEstimate(
            flops=4 * n * half * depth * share,
            bytes_accessed=4 * n * half * share * 2,
            transcendentals=half * share,
        ),
    )(pool_taps, cot_taps, enc_mat, dec_mat)


def wide_shards(inputs, enc_weight, dec_weight, cotangent):
    parts = lax.axis_size("seq")
    rows, width = inputs.shape
    half = rows // 2
    total = half * parts
    block, taps, share = enc_weight.shape
    half_width = cotangent.shape[1]

    pooled = (inputs.astype(F32).reshape(half, 2, width).sum(axis=1) * 0.5).astype(BF16)
    cot_full = lax.all_gather(cotangent, "chan", axis=1, tiled=True)
    core = lax.axis_index("chan")
    cores = lax.axis_size("chan")
    few = half // cores
    leaving = jnp.concatenate(
        [
            lax.dynamic_slice_in_dim(pooled, core * few, few, 0),
            lax.dynamic_slice_in_dim(cot_full, core * 2 * few, 2 * few, 0),
        ],
        axis=0,
    )
    columns = to_columns(leaving, parts).reshape(parts, 1, 3 * few, block)
    columns = lax.all_gather(columns, "chan", axis=1, tiled=True)
    pool_col = columns[:, :, :few].reshape(total, block)
    cot_col = columns[:, :, few:].reshape(total, 2, block).astype(F32)
    even = cot_col[:, 0]
    odd = cot_col[:, 1]
    pair = (even + odd).astype(BF16)
    cross = (odd + shift(even, 1)).astype(BF16)
    before = jnp.concatenate([even[:1].astype(BF16), cross[:-1]], axis=0)
    pool_taps = jnp.concatenate([shift(pool_col, t - 2) for t in range(taps)], axis=1)
    cot_taps = jnp.concatenate([shift(pair, 1), cross, pair, before, shift(pair, -1)], axis=1)
    enc_mat = enc_weight.transpose(1, 0, 2).reshape(taps * block, share)
    dec_mat = dec_weight.transpose(1, 0, 2).reshape(taps * block, share)

    joint = ring(
        pool_taps.reshape(parts, half, taps * block),
        cot_taps.reshape(parts, half, taps * block),
        enc_mat,
        dec_mat,
        parts,
    ).reshape(total, 2 * share)
    hidden_all = joint[:, :share]
    grad_all = joint[:, share:]

    contract_rows = (((0,), (0,)), ((), ()))
    contract_last = (((1,), (1,)), ((), ()))
    dec_grad = lax.dot_general(cot_taps, hidden_all, contract_rows, preferred_element_type=F32)
    enc_grad = lax.dot_general(pool_taps, grad_all, contract_rows, preferred_element_type=F32)
    dec_grad = dec_grad.astype(BF16).reshape(taps, block, share).transpose(1, 0, 2)
    enc_grad = enc_grad.astype(BF16).reshape(taps, block, share).transpose(1, 0, 2)

    dec_out = lax.dot_general(hidden_all, dec_mat, contract_last, preferred_element_type=F32)
    p0, p1, p2, p3, p4 = [dec_out[:, t * block : (t + 1) * block] for t in range(taps)]
    after4 = shift(p4, 1)
    before0 = shift(p0, -1)
    dec_even = before0 + shift(p1, -1) + p2 + p3 + after4
    dec_odd = before0 + p1 + p2 + shift(p3, 1) + after4
    decoded = jnp.stack([dec_even, dec_odd], axis=1).astype(BF16).reshape(parts, rows, block)
    enc_out = lax.dot_general(grad_all, enc_mat, contract_last, preferred_element_type=F32)
    pool_grad = sum(shift(enc_out[:, t * block : (t + 1) * block], 2 - t) for t in range(taps))
    pool_grad = pool_grad.astype(BF16).reshape(parts, half, block)
    mine = jnp.concatenate([decoded, pool_grad], axis=1)
    mine = lax.psum_scatter(mine, "chan", scatter_dimension=1, tiled=True)
    mine = lax.all_gather(to_rows(mine), "chan", axis=0, tiled=True)
    col_start = core * half_width
    mine = lax.dynamic_slice_in_dim(mine, col_start, half_width, 1).astype(F32)

    skip = lax.dynamic_slice_in_dim(inputs, col_start, half_width, 1)
    mixed_out = (skip.astype(F32) + mine[:rows]).astype(BF16)
    input_grad = (cotangent.astype(F32) + 0.5 * jnp.repeat(mine[rows:], 2, axis=0)).astype(BF16)
    return mixed_out, input_grad, enc_grad, dec_grad


PAD = 8
LANES = 128


def whole_kernel(
    n, own_ref, enc_ref, dec_ref, enc_grad_ref, dec_grad_ref, out_ref, gathered,
    both, padded, x_ref, y_ref, slots, term, mine, stage, acc, leaving, arriving, settled, landed,
    enc_sum, dec_sum, rs_send, rs_recv, ag_send, ag_recv, local_sem, stage_sem,
    out_send, out_recv, pair_send, pair_recv, back_send, back_recv, sum_send, sum_recv, last_send, last_recv,
):
    me = lax.axis_index("seq")
    core = lax.axis_index("chan")
    place = ring_place(me, n)
    nexts = (ring_index(place + 1, n), ring_index(place - 1, n))
    few, block = own_ref.shape[1] // 3, own_ref.shape[2]
    half = 2 * few
    share = enc_ref.shape[1]
    side = half // 2
    piece = side // PIECES
    mesh_ids = pl.DeviceIdType.MESH

    barrier = pltpu.get_barrier_semaphore()
    around = [i if up else -i for i in range(1, n // 2 + 1) for up in (True, False)][: n - 1]
    others = [ring_index(place + i, n) for i in around]
    sources = [ring_index(place - i, n) for i in around]
    for other in others:
        pl.semaphore_signal(barrier, inc=1, device_id={"seq": other}, device_id_type=mesh_ids)
    pl.semaphore_signal(barrier, inc=1, device_id={"chan": 1 - core}, device_id_type=mesh_ids)
    pl.semaphore_wait(barrier, n)

    def remote(src, dst, send, recv, where):
        return pltpu.make_async_remote_copy(
            src_ref=src,
            dst_ref=dst,
            send_sem=send,
            recv_sem=recv,
            device_id=where,
            device_id_type=mesh_ids,
        )

    other_core = {"chan": 1 - core}

    def out_copy(i):
        return remote(
            own_ref.at[others[i]], both.at[core, me], out_send.at[i], out_recv.at[i], {"seq": others[i]}
        )

    def pair_copy(i, chunk, part):
        block_of = both.at[part, chunk]
        return remote(block_of, block_of, pair_send.at[i], pair_recv.at[i], other_core)

    for i in range(n - 1):
        out_copy(i).start()
    keep = pltpu.make_async_copy(own_ref.at[me], both.at[core, me], local_sem)
    keep.start()
    padded[...] = jnp.zeros_like(padded)
    x_ref[...] = jnp.zeros_like(x_ref)
    y_ref[...] = jnp.zeros_like(y_ref)
    acc[...] = jnp.zeros_like(acc)
    enc_sum[...] = jnp.zeros_like(enc_sum)
    dec_sum[...] = jnp.zeros_like(dec_sum)
    keep.wait()
    pair_copy(n - 1, me, core).start()
    for i in range(n - 1):
        remote(
            own_ref.at[me], both.at[core, sources[i]], out_send.at[i], out_recv.at[i], {"seq": others[i]}
        ).wait_recv()
        pair_copy(i, sources[i], core).start()
    pair_copy(n - 1, me, 1 - core).wait_recv()
    for i in range(n - 1):
        pair_copy(i, sources[i], 1 - core).wait_recv()

    def widen(chunk, carry):
        for part in range(2):
            for k in range(3):
                at = pl.ds(pl.multiple_of(PAD + chunk * half + part * few, 8), few)
                padded[k, at, :block] = both[part, chunk, k * few : (k + 1) * few].astype(F32)
        return carry

    lax.fori_loop(0, n, widen, 0)

    def taps_of(chunk, carry):
        def rows(k, by):
            return padded[k, pl.ds(chunk * half + (PAD + by), half), :block]

        for t in range(5):
            x_ref[chunk, :, t * LANES : t * LANES + block] = rows(0, t - 2).astype(BF16)
        for t, (a, b) in enumerate(((1, 1), (1, 0), (0, 0), (0, -1), (-1, -1))):
            both_rows = rows(1, a) + rows(2, b)
            y_ref[chunk, :, t * LANES : t * LANES + block] = both_rows.astype(BF16)
        return carry

    lax.fori_loop(0, n, taps_of, 0)

    def signed(d, steps):
        return place - steps if d == 0 else place + steps

    def own_term(d, steps):
        chunk = ring_index(signed(d, steps), n)
        at = pl.ds(d * side, side)
        a = jnp.dot(x_ref[chunk, at, :], enc_ref[...], preferred_element_type=F32)
        b = jnp.dot(y_ref[chunk, at, :], dec_ref[...], preferred_element_type=F32)
        return a, b

    def rs_copy(d, s, q):
        at = pl.ds(q * piece, piece)
        return pltpu.make_async_remote_copy(
            src_ref=slots.at[d, s, at],
            dst_ref=slots.at[d, s + 1, at],
            send_sem=rs_send.at[d, s, q],
            recv_sem=rs_recv.at[d, s, q],
            device_id={"seq": nexts[d]},
            device_id_type=mesh_ids,
        )

    def ag_copy(d, s, q, first, owner_steps):
        at = pl.ds(d * side + q * piece, piece)
        owner = ring_index(signed(d, owner_steps), n)
        return pltpu.make_async_remote_copy(
            src_ref=mine.at[at] if first else gathered.at[owner, at],
            dst_ref=gathered.at[owner, at],
            send_sem=ag_send.at[d, s, q],
            recv_sem=ag_recv.at[d, s, q],
            device_id={"seq": nexts[d]},
            device_id_type=mesh_ids,
        )

    for d in range(2):
        a, b = own_term(d, 1)
        slots[d, 0, :, :share] = a.astype(BF16)
        slots[d, 0, :, share:] = b.astype(BF16)
        for q in range(PIECES):
            rs_copy(d, 0, q).start()

    def fill(s):
        for d in range(2):
            a, b = own_term(d, s + 2)
            term[d, :, :share] = a
            term[d, :, share:] = b

    def rs_step(s, carry):
        fill(s)
        for q in range(PIECES):
            at = pl.ds(q * piece, piece)
            for d in range(2):
                rs_copy(d, s, q).wait_recv()
                summed = slots[d, s + 1, at, :].astype(F32) + term[d, at, :]
                slots[d, s + 1, at, :] = summed.astype(BF16)
                rs_copy(d, s + 1, q).start()
        return carry

    lax.fori_loop(0, n - 2, rs_step, 0)
    fill(n - 2)
    for q in range(PIECES):
        at = pl.ds(q * piece, piece)
        for d in range(2):
            rs_copy(d, n - 2, q).wait_recv()
            rows = pl.ds(d * side + q * piece, piece)
            pre = slots[d, n - 1, at, :share].astype(F32) + term[d, at, :share]
            grad = slots[d, n - 1, at, share:].astype(F32) + term[d, at, share:]
            value, slope = gelu_and_slope(pre)
            mine[rows, :share] = value.astype(BF16)
            mine[rows, share:] = (grad * slope).astype(BF16)
            ag_copy(d, 0, q, True, 0).start()

    contract_rows = (((0,), (0,)), ((), ()))
    contract_last = (((1,), (1,)), ((), ()))

    def consume(chunk, d, load):
        at = pl.ds(d * side, side)
        hid = load(slice(None, share))
        pre_grad = load(slice(share, None))
        dec_sum[...] += lax.dot_general(
            y_ref[chunk, at, :], hid, contract_rows, preferred_element_type=F32
        )
        enc_sum[...] += lax.dot_general(
            x_ref[chunk, at, :], pre_grad, contract_rows, preferred_element_type=F32
        )
        p = lax.dot_general(hid, dec_ref[...], contract_last, preferred_element_type=F32)
        g = lax.dot_general(pre_grad, enc_ref[...], contract_last, preferred_element_type=F32)
        p = [p[:, t * LANES : (t + 1) * LANES] for t in range(5)]
        base = chunk * half + (PAD + d * side)

        def add(k, by, what):
            to = pl.ds(base + by, side)
            acc[k, to, :] += what

        add(1, 1, p[0] + p[1])
        add(1, 0, p[2] + p[3])
        add(1, -1, p[4])
        add(2, 1, p[0])
        add(2, 0, p[1] + p[2])
        add(2, -1, p[3] + p[4])
        for t in range(5):
            add(0, t - 2, g[:, t * LANES : (t + 1) * LANES])

    def stage_copy(d, s):
        owner = ring_index(signed(d, s + 1), n)
        return pltpu.make_async_copy(
            gathered.at[owner, pl.ds(d * side, side)], stage.at[d], stage_sem.at[d]
        )

    def take(d, s):
        stage_copy(d, s).wait()
        consume(ring_index(signed(d, s + 1), n), d, lambda cols: stage[d, :, cols])

    def pass_on(s, q):
        for d in range(2):
            ag_copy(d, s, q, True, s + 1).wait_recv()
            ag_copy(d, s + 1, q, False, s + 1).start()

    for q in range(PIECES):
        pass_on(0, q)
        consume(me, q, lambda cols: mine[q * side : (q + 1) * side, cols])

    def ag_step(s, carry):
        for d in range(2):
            stage_copy(d, s - 1).start()
        for q in range(PIECES):
            pass_on(s, q)
            take(q, s - 1)
        return carry

    lax.fori_loop(1, n - 2, ag_step, 0)
    for d in range(2):
        stage_copy(d, n - 3).start()
    for q in range(PIECES):
        for d in range(2):
            ag_copy(d, n - 2, q, True, n - 1).wait_recv()
        take(q, n - 3)
    for d in range(2):
        stage_copy(d, n - 2).start()
    for d in range(2):
        take(d, n - 2)

    def pick(k, chunk, part):
        at = pl.ds(pl.multiple_of(PAD + chunk * half + part * few, 8), few)
        return acc[k, at, :block]

    def sum_copy(i, chunk):
        return remote(leaving.at[chunk], arriving.at[chunk], sum_send.at[i], sum_recv.at[i], other_core)

    def back_copy(i, to, at):
        return remote(settled.at[to], landed.at[at], back_send.at[i], back_recv.at[i], {"seq": others[i]})

    order = others + [me]
    for i in range(n):
        for k in range(3):
            leaving[order[i], k * few : (k + 1) * few] = pick(k, order[i], 1 - core).astype(BF16)
        sum_copy(i, order[i]).start()
    for i in range(n):
        chunk = order[i]
        sum_copy(i, chunk).wait_recv()
        for k in range(3):
            at = slice(k * few, (k + 1) * few)
            summed = pick(k, chunk, core) + arriving[chunk, at].astype(F32)
            settled[chunk, at] = summed.astype(BF16)
        if i < n - 1:
            back_copy(i, chunk, me).start()
    keep_back = pltpu.make_async_copy(settled.at[me], landed.at[me], local_sem)
    keep_back.start()
    enc_grad_ref[...] = enc_sum[...].astype(BF16)
    dec_grad_ref[...] = dec_sum[...].astype(BF16)

    def drain(s, carry):
        for q in range(PIECES):
            for d in range(2):
                rs_copy(d, s, q).wait_send()
                ag_copy(d, s, q, True, s).wait_send()
        return carry

    lax.fori_loop(0, n - 1, drain, 0)
    for i in range(n):
        pair_copy(i, me, core).wait_send()
        sum_copy(i, me).wait_send()
    for i in range(n - 1):
        out_copy(i).wait_send()
    keep_back.wait()
    for i in range(n - 1):
        back_copy(i, me, sources[i]).wait_recv()
    theirs = landed.at[pl.ds((1 - core) * (n // 2), n // 2)]
    last = remote(theirs, out_ref.at[core], last_send, last_recv, other_core)
    last.start()
    ours = pltpu.make_async_copy(
        landed.at[pl.ds(core * (n // 2), n // 2)], out_ref.at[core], local_sem
    )
    ours.start()
    for i in range(n - 1):
        back_copy(i, me, me).wait_send()
    ours.wait()
    last.wait()


def whole_ring(own, enc_mat, dec_mat):
    n, triple, block = own.shape
    half = triple // 3 * 2
    depth, share = enc_mat.shape
    vmem = pl.BlockSpec(memory_space=pltpu.VMEM)
    steps = (2, n - 1, PIECES)
    dma = pltpu.SemaphoreType.DMA
    return pl.pallas_call(
        functools.partial(whole_kernel, n),
        out_shape=[
            jax.ShapeDtypeStruct((depth, share), BF16),
            jax.ShapeDtypeStruct((depth, share), BF16),
            jax.ShapeDtypeStruct((2, n // 2, triple, block), BF16),
            jax.ShapeDtypeStruct((n, half, 2 * share), BF16),
        ],
        in_specs=[vmem] * 3,
        out_specs=[vmem] * 3 + [pl.BlockSpec(memory_space=pl.ANY)],
        scratch_shapes=[
            pltpu.VMEM((2,) + own.shape, BF16),
            pltpu.VMEM((3, n * half + 2 * PAD, LANES), F32),
            pltpu.VMEM((n, half, depth), BF16),
            pltpu.VMEM((n, half, depth), BF16),
            pltpu.VMEM((2, n, half // 2, 2 * share), BF16),
            pltpu.VMEM((2, half // 2, 2 * share), F32),
            pltpu.VMEM((half, 2 * share), BF16),
            pltpu.VMEM((2, half // 2, 2 * share), BF16),
            pltpu.VMEM((3, n * half + 2 * PAD, LANES), F32),
            pltpu.VMEM(own.shape, BF16),
            pltpu.VMEM(own.shape, BF16),
            pltpu.VMEM(own.shape, BF16),
            pltpu.VMEM(own.shape, BF16),
            pltpu.VMEM((depth, share), F32),
            pltpu.VMEM((depth, share), F32),
            dma(steps), dma(steps), dma(steps), dma(steps), dma, dma((2,)),
            dma((n,)), dma((n,)), dma((n,)), dma((n,)), dma((n,)), dma((n,)), dma((n,)), dma((n,)), dma, dma,
        ],
        compiler_params=pltpu.CompilerParams(
            collective_id=0, has_side_effects=True, vmem_limit_bytes=56 * 2**20
        ),
        cost_estimate=pl.CostEstimate(
            flops=12 * n * half * depth * share,
            bytes_accessed=8 * n * half * share,
            transcendentals=half * share,
        ),
    )(own, enc_mat, dec_mat)[:3]


def shards(inputs, enc_weight, dec_weight, cotangent):
    parts = lax.axis_size("seq")
    cores = lax.axis_size("chan")
    rows, width = inputs.shape
    half = rows // 2
    few = half // 2
    block, taps, share = enc_weight.shape
    half_width = cotangent.shape[1]
    if cores != 2 or taps != 5 or block > LANES or parts * half > 2048 or parts % 2 or parts < 4:
        return wide_shards(inputs, enc_weight, dec_weight, cotangent)
    core = lax.axis_index("chan")

    some = lax.dynamic_slice_in_dim(inputs, core * half, half, 0)
    pooled = (some.astype(F32).reshape(few, 2, width).sum(axis=1) * 0.5).astype(BF16)
    cot_full = lax.all_gather(cotangent, "chan", axis=1, tiled=True)
    cot_some = lax.dynamic_slice_in_dim(cot_full, core * half, half, 0).reshape(few, 2, width)
    leaving = jnp.concatenate([pooled, cot_some[:, 0], cot_some[:, 1]], axis=0)
    columns = leaving.reshape(3 * few, parts, block).transpose(1, 0, 2)

    def matrix(weight):
        fill = ((0, 0), (0, LANES - block), (0, 0))
        return jnp.pad(weight.transpose(1, 0, 2), fill).reshape(taps * LANES, share)

    enc_grad, dec_grad, back = whole_ring(columns, matrix(enc_weight), matrix(dec_weight))

    def unfold(grad):
        return grad.reshape(taps, LANES, share)[:, :block].transpose(1, 0, 2)

    col_start = core * half_width
    mine = back.astype(F32).transpose(0, 2, 1, 3).reshape(2, 3, few, half_width)
    pool_grad = mine[:, 0].reshape(half, half_width)
    decoded = jnp.stack([mine[:, 1], mine[:, 2]], axis=2).reshape(rows, half_width)
    skip = lax.dynamic_slice_in_dim(inputs, col_start, half_width, 1)
    mixed_out = (skip.astype(F32) + decoded).astype(BF16)
    input_grad = (cotangent.astype(F32) + 0.5 * jnp.repeat(pool_grad, 2, axis=0)).astype(BF16)
    return mixed_out, input_grad, unfold(enc_grad), unfold(dec_grad)


def solution(mesh):
    return jax.shard_map(
        shards,
        mesh=mesh,
        in_specs=(
            P(("groups", "seq"), None),
            P("seq", None, "chan"),
            P("seq", None, "chan"),
            P(("groups", "seq"), "chan"),
        ),
        out_specs=(
            P(("groups", "seq"), "chan"),
            P(("groups", "seq"), "chan"),
            P(("groups", "seq"), None, "chan"),
            P(("groups", "seq"), None, "chan"),
        ),
        check_vma=False,
    )
```
